32 devices in a mesh: grp: 2 (over y), tchunk: 2 (over x), ha: 4 (over z), wa: 2 (over core).
Axes of the slice: x: 2, y: 2, z: 4, core: 2. Of those that a mesh axis runs over, the one named last changes fastest.
Arguments:
- features: bfloat16 [32, 32, 16, 192], P(('grp', 'tchunk'), 'ha', 'wa'), parts along dimension 0, may hold values from -6 to 6
- frame_counts: int32 [4], P(('grp', 'tchunk')), parts along dimension 0, may hold values from 0 to 8, as said below
- gain_first: float32 [192], replicated, may hold values from 0.25 to 1.75
- conv_first: bfloat16 [3, 3, 3, 192, 192], replicated, may hold values from -0.078125 to 0.078125
- bias_first: float32 [192], replicated, may hold values from -1.8 to 1.8
- gain_second: float32 [192], replicated, may hold values from 0.25 to 1.75
- conv_second: bfloat16 [3, 3, 3, 192, 192], replicated, may hold values from -0.078125 to 0.078125
- bias_second: float32 [192], replicated, may hold values from -1.8 to 1.8
Outputs:
- decoded: bfloat16 [32, 32, 16, 192], P(('grp', 'tchunk'), 'ha', 'wa'), parts along dimension 0
The draws below stay inside these ranges and needn't reach their ends.
There are 2 independent parts, one for each index of `grp`. The reference program is written for one: setup_inputs(seed, part) draws one part's arguments, and reference() takes and returns one part's arrays. A program takes and returns all parts, laid end to end along the dimension named above; an argument that names none is the same for every part. Nothing has to cross between parts.
Inputs may be any that keep to these rules, and one draw needn't show every extreme that they name: `frame_counts`: in every draw some temporal block has all 8 slots live; any block may have none.
All inputs are finite; a program needn't handle non-finite values.
Results may differ from the reference program's by a relative error of at most 0.0039.
Values may be sent and summed in bfloat16 or wider, within the bound.
A program may use at most 64 MiB of HBM per device.

```python
import jax
import jax.numpy as jnp
from jax import lax

C = 192
F = 8
FRAMES = 16
HEIGHT = 32
WIDTH = 16
N_TCHUNK = 2


def draw_frame_counts(key, part):
    totals = jax.random.randint(key, (N_TCHUNK,), 0, F + 1)
    chosen = jax.random.randint(jax.random.fold_in(key, 11), (), 0, N_TCHUNK)
    return jnp.where(jnp.arange(N_TCHUNK) == chosen, F, totals).astype(jnp.int32)


def block_scale(rng, extent, shards, low, largest):
    loudness, own = 1.0, jax.random.fold_in(rng, 6)
    for position, blocks in shards:
        heights = jnp.exp(jax.random.uniform(jax.random.fold_in(own, position), (blocks,), jnp.float32, low / len(shards), largest / len(shards)))
        loudness = loudness * jnp.repeat(heights, extent[position] // blocks).reshape([-1 if axis == position else 1 for axis in range(len(extent))])
    return loudness


def bell_draw(key, extent, spread, reach, cuts=(), held_as=jnp.bfloat16):
    values = spread * jax.random.normal(key, extent, jnp.float32)
    if cuts:
        values = values * block_scale(key, extent, cuts, -0.22, 0.18)
    return jnp.clip(values, -reach, reach).astype(held_as)


def setup_inputs(seed: int = 0, part: int = 0) -> dict:
    key_of = jax.random.split(jax.random.key(seed), 9)
    own_keys = jax.random.split(jax.random.fold_in(key_of[8], part), 9)
    return {
        "features": bell_draw(own_keys[0], (FRAMES, HEIGHT, WIDTH, C), 1.0, 6.0, ((0, 2), (1, 4), (2, 2))),
        "frame_counts": draw_frame_counts(jax.random.fold_in(jax.random.fold_in(key_of[8], part), 71), part),
        "gain_first": jnp.clip(1.0 + 0.15 * jax.random.normal(key_of[2], (C,), jnp.float32), 0.25, 1.75),
        "conv_first": bell_draw(key_of[3], (3, 3, 3, C, C), (27 * C) ** -0.5, 0.078125),
        "bias_first": bell_draw(key_of[4], (C,), 0.3, 1.8, (), jnp.float32),
        "gain_second": jnp.clip(1.0 + 0.15 * jax.random.normal(key_of[5], (C,), jnp.float32), 0.25, 1.75),
        "conv_second": bell_draw(key_of[6], (3, 3, 3, C, C), (27 * C) ** -0.5, 0.078125),
        "bias_second": bell_draw(key_of[7], (C,), 0.3, 1.8, (), jnp.float32),
    }


epsilon = 1e-06

def activate(values, gain):
    values = values.astype(jnp.float32)
    inverse = lax.rsqrt(lax.optimization_barrier(jnp.mean(values * values, axis=-1, keepdims=True)) + epsilon)
    return jax.nn.silu(values * inverse * gain).astype(jnp.bfloat16)

def convolve(stacked, kernel, bias_term):
    padded = jnp.pad(stacked.astype(jnp.float32), ((0, 0), (1, 1), (1, 1), (0, 0)))
    result = lax.conv_general_dilated(padded[None], kernel.astype(jnp.float32), (1, 1, 1), 'VALID', dimension_numbers=('NDHWC', 'DHWIO', 'NDHWC'), precision=lax.Precision.HIGHEST)
    return result[0] + bias_term

def reference(features, frame_counts, gain_first, conv_first, bias_first, gain_second, conv_second, bias_second):
    blocks = features.reshape(N_TCHUNK, F, HEIGHT, WIDTH, C)

    def advance(carry, inputs):
        cache_first, cache_second = carry
        block_frames, frame_total = inputs
        valid_mask = (jnp.arange(F) < frame_total)[:, None, None, None]
        first_input = jnp.where(valid_mask, activate(block_frames, gain_first), jnp.zeros_like(block_frames))
        joined_first = jnp.concatenate([cache_first, first_input], axis=0)
        hidden = convolve(joined_first, conv_first, bias_first)
        second_input = jnp.where(valid_mask, activate(hidden, gain_second), jnp.zeros_like(block_frames))
        joined_second = jnp.concatenate([cache_second, second_input], axis=0)
        result = convolve(joined_second, conv_second, bias_second)
        outcome = jnp.where(valid_mask, block_frames.astype(jnp.float32) + result, jnp.zeros((), jnp.float32)).astype(jnp.bfloat16)
        start = frame_total.astype(jnp.int32)
        new_first = lax.dynamic_slice_in_dim(joined_first, start, 2, 0)
        new_second = lax.dynamic_slice_in_dim(joined_second, start, 2, 0)
        return ((new_first, new_second), outcome)
    empty = jnp.zeros((2, HEIGHT, WIDTH, C), jnp.bfloat16)
    final_caches, decoded = lax.scan(advance, (empty, empty), (blocks, frame_counts))
    return decoded.reshape(FRAMES, HEIGHT, WIDTH, C)
```

```python
import functools

import jax
import jax.numpy as jnp
from jax import lax
from jax.experimental import pallas as pl
from jax.experimental.pallas import tpu as pltpu
from jax.sharding import PartitionSpec as P

epsilon = 1e-06
MESH = pl.DeviceIdType.MESH
LANES = 128
f32, bf16 = jnp.float32, jnp.bfloat16


def silu_norm(values, gain):
    inverse = lax.rsqrt(jnp.mean(values * values, axis=-1, keepdims=True) + epsilon)
    return jax.nn.silu(values * inverse * gain)


def kernel(sizes, *refs):
    placed, out, scratch = refs[:8], refs[8], refs[9:]
    n_t, n_z, n_w = sizes
    cnt_ref, feat_hbm, g1_hbm, w1_hbm, b1_hbm, g2_hbm, w2_hbm, b2_hbm = placed
    (feat, g1, b1, g2, b2, wl1, wc1, ws1, wl2, wc2, ws2, lsem, lo, hc, hs, acc,
     clo, chc, chs, cnt_own, cnt_in, carry, carry_col, csend, crecv) = scratch[:25]
    one, two = scratch[25:37], scratch[37:49]
    F, R, X, C = feat.shape
    H = F // 2
    S = F * X
    T = 2 * X
    me_t, me_z, me_w = lax.axis_index("tchunk"), lax.axis_index("ha"), lax.axis_index("wa")
    left_core = me_w == 0
    has = (me_z > 0, me_z < n_z - 1)
    frame_of = [(g % 2) * H + g // 2 for g in range(F)]

    def load(i, src, dst):
        return pltpu.make_async_copy(src, dst, lsem.at[i])

    def weight_loads(i, w, wl, wc, ws):
        low, high = pl.ds(0, LANES), pl.ds(LANES, C - LANES)
        top, bottom = pl.ds(0, C - LANES), pl.ds(C - LANES, C - LANES)
        return [
            load(i, w.at[:, :, :, low], wl),
            load(i + 1, w.at[0, :, 1, high], wc.at[0, :, top]),
            load(i + 2, w.at[1, :, 1, high], wc.at[0, :, bottom]),
            load(i + 3, w.at[2, :, 1, high], wc.at[1, :, top]),
            load(i + 4, w.at[:, :, 0, high], ws.at[:, :, top]),
            load(i + 5, w.at[:, :, 2, high], ws.at[:, :, bottom]),
        ]

    load_feat = load(0, feat_hbm, feat)
    load_g1 = load(1, g1_hbm, g1)
    load_rest = [load(2, b1_hbm, b1), load(3, g2_hbm, g2), load(4, b2_hbm, b2)]
    load_w1 = weight_loads(5, w1_hbm, wl1, wc1, ws1)
    load_w2 = weight_loads(11, w2_hbm, wl2, wc2, ws2)
    load_feat.start()
    load_g1.start()

    def device(k, dz, flip):
        return {
            "tchunk": k,
            "ha": lax.rem(me_z + dz + n_z, n_z),
            "wa": 1 - me_w if flip else me_w,
        }

    barrier = pltpu.get_barrier_semaphore()
    pl.semaphore_signal(barrier, inc=1, device_id=device(me_t, 0, True), device_id_type=MESH)
    for side in range(2):
        @pl.when(has[side])
        def _(side=side):
            for flip in (False, True):
                pl.semaphore_signal(
                    barrier, inc=1, device_id=device(me_t, 2 * side - 1, flip), device_id_type=MESH
                )
    for k in range(n_t):
        @pl.when(me_t != k)
        def _(k=k):
            pl.semaphore_signal(barrier, inc=1, device_id=device(k, 0, False), device_id_type=MESH)
    expected = n_t + 2 * has[0].astype(jnp.int32) + 2 * has[1].astype(jnp.int32)

    for c in load_w1 + load_rest + load_w2:
        c.start()

    def near(bufs, which, way=1):
        rows, col_out, row_in, col_in, _, _, _, _, ssem, rsem = bufs[:10]
        if which == 4:
            src, dst, dz, flip = col_out, col_in.at[pl.ds(1, R)], 0, True
        else:
            side, flip = which % 2, which >= 2
            dz = 2 * side - 1
            y, yy = (0, R + 1) if side == 0 else (R - 1, 0)
            if flip:
                src, dst = col_out.at[y], col_in.at[yy]
            else:
                src, dst = rows.at[y], row_in.at[1 - side]
        return pltpu.make_async_remote_copy(
            src, dst, ssem.at[which], rsem.at[which], device_id=device(me_t, way * dz, flip), device_id_type=MESH
        )

    def far(bufs, k, slot, which):
        _, _, _, _, tail, tailc, tail_in, tailc_in, _, _, ssem, rsem = bufs
        if which == 0:
            src, dst = tail.at[pl.ds(1, R)], tail_in.at[slot, pl.ds(1, R)]
        elif which == 3:
            src, dst = tailc, tailc_in.at[slot]
        else:
            yy = 0 if which == 1 else R + 1
            src, dst = tail.at[yy], tail_in.at[slot, yy]
        return pltpu.make_async_remote_copy(
            src, dst, ssem.at[k, which], rsem.at[slot, which],
            device_id=device(k, 0, False), device_id_type=MESH,
        )

    def count_copy(k, slot):
        return pltpu.make_async_remote_copy(
            cnt_own, cnt_in.at[slot], csend.at[k], crecv.at[slot],
            device_id=device(k, 0, False), device_id_type=MESH,
        )

    def later(act):
        for k in range(1, n_t):
            @pl.when(me_t < k)
            def _(k=k):
                act(k)

    def clear(bufs):
        row_in, col_in = bufs[2], bufs[3]
        for side in range(2):
            @pl.when(jnp.logical_not(has[side]))
            def _(side=side):
                row_in[side] = jnp.zeros((S, C), bf16)
                col_in[side * (R + 1)] = jnp.zeros((F, C), bf16)

    clear(one)
    clear(two)
    for wc in (wc1, wc2):
        wc[1, :, C - LANES :] = jnp.zeros((3, C - LANES, C), bf16)

    count = cnt_ref[0]
    cnt_own[...] = jnp.full(cnt_own.shape, count.astype(f32), f32)
    group = lax.broadcasted_iota(jnp.int32, (F, X, C), 0)
    live = lax.rem(group, 2) * H + group // 2 < count
    xi = lax.broadcasted_iota(jnp.int32, (F, X, C), 1)

    def tail_of(v):
        got = []
        for f in range(2):
            t = jnp.zeros((X, C), f32)
            for g in range(F):
                t = jnp.where(count - 2 + f == frame_of[g], v[g], t)
            got.append(t)
        return jnp.concatenate(got, axis=0).astype(bf16)

    def keep(bufs, y, v):
        rows, col_out, tail = bufs[0], bufs[1], bufs[4]
        v = jnp.where(live, v.reshape(F, X, C), 0.0)
        rows[y] = v.reshape(S, C).astype(bf16)
        col_out[y] = jnp.where(left_core, v[:, X - 1, :], v[:, 0, :]).astype(bf16)
        if n_t > 1:
            tail[y + 1] = tail_of(v)

    def shifted(v, col):
        index = lax.broadcasted_iota(jnp.int32, v.shape, 1)
        none = jnp.zeros(col.shape, f32)
        lcol = jnp.where(left_core, none, col)
        rcol = jnp.where(left_core, col, none)
        left = jnp.where(index == 0, jnp.broadcast_to(lcol[:, None, :], v.shape), pltpu.roll(v, 1, 1))
        right = jnp.where(index == X - 1, jnp.broadcast_to(rcol[:, None, :], v.shape), pltpu.roll(v, X - 1, 1))
        return left, v, right

    def assemble(yy, v, col):
        zero = jnp.zeros((X, C), f32)
        made = []
        for j, b in enumerate(shifted(v.reshape(F, X, C), col)):
            front = jnp.concatenate([zero, b[2 * (H - 2)], zero, b[2 * (H - 1)]], axis=0)
            t = jnp.concatenate([front, b.reshape(S, C)], axis=0).astype(bf16)
            lo[j, yy] = t[:, :LANES]
            made.append(t[:, LANES:])
        hs[yy] = jnp.concatenate([made[0], made[2]], axis=1)
        after = jnp.concatenate([made[1][T:], jnp.zeros((T, C - LANES), bf16)], axis=0)
        hc[yy] = jnp.concatenate([made[1], after], axis=1)

    def conv(i, y0, y1, wl, wc, ws, first=False):
        n = y1 - y0

        def take(ref, a):
            return ref[pl.ds(y0 + i, n), pl.ds(a * T, S)].reshape(n * S, LANES)

        lhs = [take(lo.at[j], a) for a in range(3) for j in range(3)]
        lhs += [take(hc, 0), take(hc, 2)] + [take(hs, a) for a in range(3)]
        rhs = [wl[a, i].reshape(3 * LANES, C) for a in range(3)]
        rhs += [wc[0, i], wc[1, i]] + [ws[a, i] for a in range(3)]
        part = jnp.dot(jnp.concatenate(lhs, axis=1), jnp.concatenate(rhs, axis=0), preferred_element_type=f32)
        at = pl.ds(y0 * S, n * S)
        if first:
            acc[at] = part
        else:
            acc[at] += part

    def early(bufs, first):
        rows, col_in = bufs[0], bufs[3]
        near(bufs, 4).wait_recv()
        for y in range(R):
            assemble(y + 1, rows[y].astype(f32), col_in[y + 1].astype(f32))

    def main(wl, wc, ws):
        conv(1, 0, R, wl, wc, ws, True)
        conv(0, 1, R, wl, wc, ws)
        conv(2, 0, R - 1, wl, wc, ws)

    def edges(bufs, wl, wc, ws):
        row_in, col_in, tail, tailc = bufs[2], bufs[3], bufs[4], bufs[5]
        for side in range(2):
            @pl.when(has[side])
            def _(side=side):
                near(bufs, 1 - side, -1).wait_recv()
                near(bufs, 3 - side, -1).wait_recv()
        if n_t > 1:
            tail[0] = tail_of(row_in[0].astype(f32).reshape(F, X, C))
            tail[R + 1] = tail_of(row_in[1].astype(f32).reshape(F, X, C))
            at = lax.broadcasted_iota(jnp.int32, (F, C), 0)
            of_row = lax.rem(at, 2) * H + at // 2
            index = lax.broadcasted_iota(jnp.int32, (tailc.shape[1], C), 0)
            for f in range(2):
                t = jnp.zeros(index.shape, f32)
                for yy in range(R + 2):
                    only = jnp.where(of_row == count - 2 + f, col_in[yy].astype(f32), 0.0)
                    t = jnp.where(index == yy, jnp.sum(only, axis=0, keepdims=True), t)
                tailc[f] = t.astype(bf16)

            def go(k):
                for which in (1, 2, 3):
                    far(bufs, k, me_t, which).start()

            later(go)
        for yy in (0, R + 1):
            assemble(yy, row_in[min(yy, 1)].astype(f32), col_in[yy].astype(f32))
        conv(0, 0, 1, wl, wc, ws)
        conv(2, R - 1, R, wl, wc, ws)

    def before(bufs, first, wl, wc, ws):
        tail_in, tailc_in = bufs[6], bufs[7]
        carry[...] = jnp.zeros(carry.shape, f32)
        carry_col[...] = jnp.zeros(carry_col.shape, f32)
        for k in range(n_t - 1):
            @pl.when(me_t > k)
            def _(k=k):
                if first:
                    count_copy(k, k).wait_recv()
                for which in range(4):
                    far(bufs, k, k, which).wait_recv()
                total = cnt_in[k]
                wide = jnp.concatenate([total] * (carry_col.shape[1] // X), axis=0)

                def merge(total, early0, early1, late0, late1):
                    both, some = total > 1.5, total > 0.5
                    return (
                        jnp.where(both, late0, jnp.where(some, early1, early0)),
                        jnp.where(some, late1, early1),
                    )

                for yy in range(R + 2):
                    late = tail_in[k, yy].astype(f32)
                    got = merge(total, carry[yy, :X], carry[yy, X:], late[:X], late[X:])
                    carry[yy] = jnp.concatenate(got, axis=0)
                got = merge(
                    wide, carry_col[0], carry_col[1], tailc_in[k, 0].astype(f32), tailc_in[k, 1].astype(f32)
                )
                carry_col[0] = got[0]
                carry_col[1] = got[1]

        cols = (carry_col[0], carry_col[1])
        zero = jnp.zeros((X, C), f32)
        for yy in range(R + 2):
            col = jnp.concatenate([c[yy : yy + 1] for c in cols], axis=0)
            made, mid = [], None
            for j, b in enumerate(shifted(carry[yy].reshape(2, X, C), col)):
                t = jnp.concatenate([b[0], b[1], b[1], zero], axis=0).astype(bf16)
                clo[j, yy] = t[:, :LANES]
                made.append(t[:, LANES:])
            chs[yy] = jnp.concatenate([made[0], made[2]], axis=1)
            chc[yy] = jnp.concatenate([made[1][:T], made[1][T:]], axis=1)
        lhs, rhs = [], []
        for i in range(3):
            for a in range(2):
                for j in range(3):
                    lhs.append(clo[j, pl.ds(i, R), pl.ds(a * T, T)].reshape(R * T, LANES))
                lhs.append(chs[pl.ds(i, R), pl.ds(a * T, T)].reshape(R * T, LANES))
                rhs += [wl[a, i].reshape(3 * LANES, C), ws[a, i]]
            lhs.append(chc[pl.ds(i, R)].reshape(R * T, LANES))
            rhs.append(wc[0, i])
        part = jnp.dot(jnp.concatenate(lhs, axis=1), jnp.concatenate(rhs, axis=0), preferred_element_type=f32)
        for y in range(R):
            for f in range(2):
                acc[pl.ds(y * S + f * T, X)] += part[y * T + f * X : y * T + (f + 1) * X]

    def phase(bufs, first, values, wl, wc, ws, loads):
        for y in (0, R - 1):
            keep(bufs, y, values(y))
        if first:
            pl.semaphore_wait(barrier, expected)
        for side in range(2):
            @pl.when(has[side])
            def _(side=side):
                near(bufs, side).start()
                near(bufs, 2 + side).start()
        for y in range(1, R - 1):
            keep(bufs, y, values(y))
        near(bufs, 4).start()

        def go(k):
            if first:
                count_copy(k, me_t).start()
            far(bufs, k, me_t, 0).start()

        later(go)
        early(bufs, first)
        for c in loads:
            c.wait()
        main(wl, wc, ws)
        edges(bufs, wl, wc, ws)
        if n_t > 1:
            @pl.when(me_t > 0)
            def _():
                before(bufs, first, wl, wc, ws)

    def finish(bufs, first):
        near(bufs, 4).wait_send()
        for side in range(2):
            @pl.when(has[side])
            def _(side=side):
                near(bufs, side).wait_send()
                near(bufs, 2 + side).wait_send()

        def done(k):
            if first:
                count_copy(k, me_t).wait_send()
            for which in range(4):
                far(bufs, k, me_t, which).wait_send()

        later(done)

    load_feat.wait()
    load_g1.wait()

    def in_groups(y):
        return jnp.concatenate([feat[t, y].astype(f32) for t in frame_of], axis=0)

    phase(one, True, lambda y: silu_norm(in_groups(y), g1[...]), wl1, wc1, ws1, load_w1)
    for c in load_rest:
        c.wait()

    def hidden(y):
        return silu_norm(acc[pl.ds(y * S, S)] + b1[...], g2[...])

    phase(two, False, hidden, wl2, wc2, ws2, load_w2)
    for y in range(R):
        result = acc[pl.ds(y * S, S)] + b2[...]
        for g in range(F):
            t = frame_of[g]
            value = feat[t, y].astype(f32) + result[g * X : (g + 1) * X]
            out[t, y] = jnp.where(live[g], value, 0.0).astype(bf16)
    finish(one, True)
    finish(two, False)


def shards(sizes, features, frame_counts, gain_first, conv_first, bias_first, gain_second, conv_second, bias_second):
    F, R, X, C = features.shape
    n_t, n_z, n_w = sizes
    assert n_w == 2 and F % 2 == 0 and F >= 4 and X == 8 and 2 * (C - LANES) == LANES and R >= 2
    H = F // 2
    S, T = F * X, 2 * X
    wide = -(-(R + 2) // 16) * 16
    dma = pltpu.SemaphoreType.DMA
    V = pltpu.VMEM
    phase = [
        V((R, S, C), bf16),
        V((R, F, C), bf16),
        V((2, S, C), bf16),
        V((R + 2, F, C), bf16),
        V((R + 2, T, C), bf16),
        V((2, wide, C), bf16),
        V((n_t, R + 2, T, C), bf16),
        V((n_t, 2, wide, C), bf16),
        dma((5,)),
        dma((5,)),
        dma((n_t, 4)),
        dma((n_t, 4)),
    ]
    weights = [V((3, 3, 3, LANES, C), bf16), V((2, 3, LANES, C), bf16), V((3, 3, LANES, C), bf16)]
    scratch = [
        V(features.shape, bf16),
        V((1, C), f32),
        V((1, C), f32),
        V((1, C), f32),
        V((1, C), f32),
        *weights,
        *weights,
        dma((17,)),
        V((3, R + 2, (H + 2) * T, LANES), bf16),
        V((R + 2, (H + 2) * T, LANES), bf16),
        V((R + 2, (H + 2) * T, LANES), bf16),
        V((R * S, C), f32),
        V((3, R + 2, 2 * T, LANES), bf16),
        V((R + 2, T, LANES), bf16),
        V((R + 2, 2 * T, LANES), bf16),
        V((X, C), f32),
        V((n_t, X, C), f32),
        V((R + 2, T, C), f32),
        V((2, wide, C), f32),
        dma((n_t,)),
        dma((n_t,)),
    ]
    return pl.pallas_call(
        functools.partial(kernel, sizes),
        out_shape=pltpu.VMEM(features.shape, features.dtype),
        in_specs=[pl.BlockSpec(memory_space=pltpu.SMEM)] + [pl.BlockSpec(memory_space=pltpu.HBM)] * 7,
        out_specs=pl.BlockSpec(memory_space=pltpu.VMEM),
        scratch_shapes=scratch + phase + phase,
        compiler_params=pltpu.CompilerParams(
            collective_id=0, has_side_effects=True, vmem_limit_bytes=58 << 20
        ),
    )(
        frame_counts,
        features,
        gain_first.reshape(1, C),
        conv_first,
        bias_first.reshape(1, C),
        gain_second.reshape(1, C),
        conv_second,
        bias_second.reshape(1, C),
    )


def solution(mesh):
    sizes = (mesh.shape["tchunk"], mesh.shape["ha"], mesh.shape["wa"])
    spec = P(("grp", "tchunk"), "ha", "wa", None)
    return jax.shard_map(
        functools.partial(shards, sizes),
        mesh=mesh,
        in_specs=(spec, P(("grp", "tchunk")), P(), P(), P(), P(), P(), P()),
        out_specs=spec,
        check_vma=False,
    )
```

```python
import functools

import jax
import jax.numpy as jnp
from jax import lax
from jax.experimental import pallas as pl
from jax.experimental.pallas import tpu as pltpu
from jax.sharding import PartitionSpec as P

epsilon = 1e-06
MESH = pl.DeviceIdType.MESH
LANES = 128
f32, bf16 = jnp.float32, jnp.bfloat16


def silu_norm(values, gain):
    inverse = lax.rsqrt(jnp.mean(values * values, axis=-1, keepdims=True) + epsilon)
    return jax.nn.silu(values * inverse * gain)


def kernel(sizes, *refs):
    placed, out, scratch = refs[:8], refs[8], refs[9:]
    n_t, n_z, n_w = sizes
    cnt_ref, feat_hbm, g1_hbm, w1_hbm, b1_hbm, g2_hbm, w2_hbm, b2_hbm = placed
    (feat, g1, b1, g2, b2, wl1, wc1, ws1, wl2, wc2, ws2, lsem, lo, hc, hs, acc,
     clo, chc, chs, cnt_own, cnt_in, carry, carry_col,
     raw_in, rows1, col_out1, col_in1, tail1, tailc1, tail_in1, tailc_in1, tailhc_in,
     rows2, col_out2, col_in2, tail2, tailc2, tail_in2, tailc_in2,
     nsend, nrecv, fsend, frecv, up, over, over_up) = scratch
    F, R, X, C = feat.shape
    H = F // 2
    S = F * X
    T = 2 * X
    me_t, me_z, me_w = lax.axis_index("tchunk"), lax.axis_index("ha"), lax.axis_index("wa")
    left_core = me_w == 0
    has = (me_z > 0, me_z < n_z - 1)
    frame_of = [(g % 2) * H + g // 2 for g in range(F)]

    def load(i, src, dst):
        return pltpu.make_async_copy(src, dst, lsem.at[i])

    def weight_loads(i, w, wl, wc, ws):
        low, high = pl.ds(0, LANES), pl.ds(LANES, C - LANES)
        top, bottom = pl.ds(0, C - LANES), pl.ds(C - LANES, C - LANES)
        return [
            load(i, w.at[:, :, :, low], wl),
            load(i + 1, w.at[0, :, 1, high], wc.at[0, :, top]),
            load(i + 2, w.at[1, :, 1, high], wc.at[0, :, bottom]),
            load(i + 3, w.at[2, :, 1, high], wc.at[1, :, top]),
            load(i + 4, w.at[:, :, 0, high], ws.at[:, :, top]),
            load(i + 5, w.at[:, :, 2, high], ws.at[:, :, bottom]),
        ]

    load_feat = load(0, feat_hbm, feat)
    load_g1 = load(1, g1_hbm, g1)
    load_rest = [load(2, b1_hbm, b1), load(3, g2_hbm, g2), load(4, b2_hbm, b2)]
    load_w1 = weight_loads(5, w1_hbm, wl1, wc1, ws1)
    load_w2 = weight_loads(11, w2_hbm, wl2, wc2, ws2)
    load_feat.start()
    load_g1.start()

    def device(k, dz, flip):
        return {
            "tchunk": k,
            "ha": lax.rem(me_z + dz + n_z, n_z),
            "wa": 1 - me_w if flip else me_w,
        }

    barrier = pltpu.get_barrier_semaphore()

    def greet(k, dz, flip):
        pl.semaphore_signal(barrier, inc=1, device_id=device(k, dz, flip), device_id_type=MESH)

    greet(me_t, 0, True)

    @pl.when(has[1])
    def _():
        greet(me_t, 1, False)
        greet(me_t, 1, True)

    for k in range(1, n_t):
        @pl.when(me_t < k)
        def _(k=k):
            greet(k, 0, False)

    expected = 1 + 2 * has[0].astype(jnp.int32) + me_t

    def tell(sem, k, dz, flip):
        pl.semaphore_signal(sem, inc=1, device_id=device(k, dz, flip), device_id_type=MESH)

    def tell_lower(sems):
        for k in range(1, n_t):
            @pl.when(me_t == k)
            def _(k=k):
                for lower in range(k):
                    tell(sems.at[k], lower, 0, False)

    for c in load_w1 + load_rest + load_w2:
        c.start()

    def remote(src, dst, ssem, rsem, to):
        return pltpu.make_async_remote_copy(src, dst, ssem, rsem, device_id=to, device_id_type=MESH)

    def row_copy(side, way=1):
        src = feat_hbm.at[:, pl.ds((R - 2) * side, 2)]
        return remote(src, raw_in.at[1 - side], nsend.at[side], nrecv.at[side], device(me_t, way * (2 * side - 1), False))

    def corner_copy(side, way=1):
        src = col_out1.at[pl.ds((R - 2) * side, 2)]
        dst = col_in1.at[pl.ds(0 if side else R + 2, 2)]
        i = 2 + side
        return remote(src, dst, nsend.at[i], nrecv.at[i], device(me_t, way * (2 * side - 1), True))

    def col_copy(first):
        src, dst, i = (col_out1, col_in1.at[pl.ds(2, R)], 4) if first else (col_out2, col_in2, 5)
        return remote(src, dst, nsend.at[i], nrecv.at[i], device(me_t, 0, True))

    def far(k, slot, i, way=1):
        src, dst, dz, flip = (
            (tail1, tail_in1.at[slot, pl.ds(0, R)], 0, False),
            (tailc1, tailc_in1.at[slot], 0, True),
            (tail1.at[pl.ds(0, 2)], tail_in1.at[slot, pl.ds(R + 2, 2)], -1, False),
            (tailc1, tailhc_in.at[slot, 1], -1, True),
            (tail1.at[pl.ds(R - 2, 2)], tail_in1.at[slot, pl.ds(R, 2)], 1, False),
            (tailc1, tailhc_in.at[slot, 0], 1, True),
            (tail2, tail_in2.at[slot], 0, False),
            (tailc2, tailc_in2.at[slot], 0, True),
            (cnt_own, cnt_in.at[slot], 0, False),
        )[i]
        return remote(src, dst, fsend.at[k, i], frecv.at[slot, i], device(k, way * dz, flip))

    def later(act):
        for k in range(1, n_t):
            @pl.when(me_t < k)
            def _(k=k):
                act(k)

    def aside(act, side):
        @pl.when(has[side])
        def _():
            for i in (2, 3) if side == 0 else (4, 5):
                act(i)

    for side in range(2):
        @pl.when(jnp.logical_not(has[side]))
        def _(side=side):
            raw_in[side] = jnp.zeros((F, 2, X, C), bf16)
            col_in1[pl.ds(side * (R + 2), 2)] = jnp.zeros((2, F, C), bf16)
            for k in range(n_t - 1):
                tail_in1[k, pl.ds(R + 2 * side, 2)] = jnp.zeros((2, T, C), bf16)
                tailhc_in[k, side] = jnp.zeros((2, R, C), bf16)
    for wc in (wc1, wc2):
        wc[1, :, C - LANES :] = jnp.zeros((3, C - LANES, C), bf16)

    count = cnt_ref[0]
    cnt_own[...] = jnp.full(cnt_own.shape, count.astype(f32), f32)
    group = lax.broadcasted_iota(jnp.int32, (F, X, C), 0)
    live = lax.rem(group, 2) * H + group // 2 < count

    def edge(v, at=0):
        return jnp.where(left_core, v[:, at + X - 1, :], v[:, at, :])

    def tail_of(v):
        got = []
        for f in range(2):
            t = jnp.zeros((X, C), f32)
            for g in range(F):
                t = jnp.where(count - 2 + f == frame_of[g], v[g], t)
            got.append(t)
        return jnp.concatenate(got, axis=0).astype(bf16)

    def put_tail_cols(tails, dst):
        v = tails[...].astype(f32)
        more = dst.shape[1] - v.shape[0]
        for f in range(2):
            c = edge(v, f * X)
            if more:
                c = jnp.concatenate([c, jnp.zeros((more, C), f32)], axis=0)
            dst[f] = c.astype(bf16)

    def tiles(b):
        zero = jnp.zeros((X, C), f32)
        front = jnp.concatenate([zero, b[2 * (H - 2)], zero, b[2 * (H - 1)]], axis=0)
        return jnp.concatenate([front, b.reshape(S, C)], axis=0).astype(bf16)

    def center(yy, v):
        t = tiles(v)
        lo[1, yy] = t[:, :LANES]
        high = t[:, LANES:]
        after = jnp.concatenate([high[T:], jnp.zeros((T, C - LANES), bf16)], axis=0)
        hc[yy] = jnp.concatenate([high, after], axis=1)

    def beside(v, col):
        index = lax.broadcasted_iota(jnp.int32, v.shape, 1)
        none = jnp.zeros(col.shape, f32)
        lcol = jnp.where(left_core, none, col)
        rcol = jnp.where(left_core, col, none)
        left = jnp.where(index == 0, jnp.broadcast_to(lcol[:, None, :], v.shape), pltpu.roll(v, 1, 1))
        right = jnp.where(index == X - 1, jnp.broadcast_to(rcol[:, None, :], v.shape), pltpu.roll(v, X - 1, 1))
        return left, right

    def sides(yy, v, col):
        left, right = beside(v, col)
        tl, tr = tiles(left), tiles(right)
        lo[0, yy] = tl[:, :LANES]
        lo[2, yy] = tr[:, :LANES]
        hs[yy] = jnp.concatenate([tl[:, LANES:], tr[:, LANES:]], axis=1)

    def grouped(ref, index):
        return jnp.concatenate([ref[(t,) + index].astype(f32)[None] for t in frame_of], axis=0)

    def as_groups(ref, y):
        return ref[y].astype(f32).reshape(F, X, C)

    def conv(y0, n, wl, wc, ws):
        def take(ref, i, a):
            return ref[pl.ds(y0 + i, n), pl.ds(a * T, S)].reshape(n * S, LANES)

        lhs, rhs = [], []
        for i in range(3):
            lhs += [take(lo.at[j], i, a) for a in range(3) for j in range(3)]
            lhs += [take(hc, i, 0), take(hc, i, 2)] + [take(hs, i, a) for a in range(3)]
            rhs += [wl[a, i].reshape(3 * LANES, C) for a in range(3)]
            rhs += [wc[0, i], wc[1, i]] + [ws[a, i] for a in range(3)]
        acc[pl.ds(y0 * S, n * S)] = jnp.dot(
            jnp.concatenate(lhs, axis=1), jnp.concatenate(rhs, axis=0), preferred_element_type=f32
        )

    def before(first, n, wl, wc, ws):
        carry[...] = jnp.zeros(carry.shape, f32)
        carry_col[...] = jnp.zeros(carry_col.shape, f32)
        for k in range(n_t - 1):
            @pl.when(me_t > k)
            def _(k=k):
                for i in (8, 0, 1) if first else (6, 7):
                    far(k, k, i).wait_recv()
                if first:
                    @pl.when(has[0])
                    def _():
                        for i in (4, 5):
                            far(k, k, i, -1).wait_recv()

                    @pl.when(has[1])
                    def _():
                        for i in (2, 3):
                            far(k, k, i, -1).wait_recv()

                total = cnt_in[k]

                def merge(total, early0, early1, late0, late1):
                    both, some = total > 1.5, total > 0.5
                    return (
                        jnp.where(both, late0, jnp.where(some, early1, early0)),
                        jnp.where(some, late1, early1),
                    )

                for at in range(n + 2):
                    late = (tail_in1 if first else tail_in2)[k, at].astype(f32)
                    got = merge(total, carry[at, :X], carry[at, X:], late[:X], late[X:])
                    carry[at] = jnp.concatenate(got, axis=0)
                cols = (tailc_in1.at[k], tailhc_in.at[k, 0], tailhc_in.at[k, 1]) if first else (tailc_in2.at[k],)
                for d, ref in enumerate(cols):
                    late = ref[...].astype(f32)
                    there = pl.ds(0, late.shape[1])
                    got = merge(total[:1], carry_col[d, 0, there], carry_col[d, 1, there], late[0], late[1])
                    carry_col[d, 0, there] = got[0]
                    carry_col[d, 1, there] = got[1]

        zero = jnp.zeros((X, C), f32)
        for yy in range(n + 2):
            at, d, y = yy, 0, yy
            if first:
                if yy < 2:
                    at, d, y = R + yy, 1, R - 2 + yy
                elif yy < R + 2:
                    at, d, y = yy - 2, 0, yy - 2
                else:
                    d, y = 2, yy - R - 2
            col = jnp.concatenate([carry_col[d, f, y : y + 1] for f in range(2)], axis=0)
            v = carry[at].reshape(2, X, C)
            left, right = beside(v, col)
            made = []
            for j, b in enumerate((left, v, right)):
                t = jnp.concatenate([b[0], b[1], b[1], zero], axis=0).astype(bf16)
                clo[j, yy] = t[:, :LANES]
                made.append(t[:, LANES:])
            chs[yy] = jnp.concatenate([made[0], made[2]], axis=1)
            chc[yy] = jnp.concatenate([made[1][:T], made[1][T:]], axis=1)
        lhs, rhs = [], []
        for i in range(3):
            for a in range(2):
                for j in range(3):
                    lhs.append(clo[j, pl.ds(i, n), pl.ds(a * T, T)].reshape(n * T, LANES))
                lhs.append(chs[pl.ds(i, n), pl.ds(a * T, T)].reshape(n * T, LANES))
                rhs += [wl[a, i].reshape(3 * LANES, C), ws[a, i]]
            lhs.append(chc[pl.ds(i, n)].reshape(n * T, LANES))
            rhs.append(wc[0, i])
        part = jnp.dot(jnp.concatenate(lhs, axis=1), jnp.concatenate(rhs, axis=0), preferred_element_type=f32)
        for y in range(n):
            for f in range(2):
                acc[pl.ds(y * S + f * T, X)] += part[y * T + f * X : y * T + (f + 1) * X]

    pl.semaphore_wait(barrier, expected)
    tell_lower(over)

    @pl.when(has[0])
    def _():
        tell(up.at[0], me_t, -1, False)
        tell(up.at[1], me_t, -1, True)
        row_copy(0).start()

    load_feat.wait()
    load_g1.wait()

    def keep_first(y):
        v = silu_norm(grouped(feat, (y,)), g1[...].reshape(1, 1, C))
        v = jnp.where(live, v, 0.0)
        rows1[y] = v.reshape(S, C).astype(bf16)
        col_out1[y] = edge(v).astype(bf16)
        if n_t > 1:
            tail1[y] = tail_of(v)
        center(y + 2, v)

    ends = sorted({0, 1, R - 2, R - 1})
    for y in ends:
        keep_first(y)

    @pl.when(has[0])
    def _():
        corner_copy(0).start()

    for y in range(R):
        if y not in ends:
            keep_first(y)
    col_copy(True).start()

    @pl.when(has[1])
    def _():
        pl.semaphore_wait(up.at[0], 1)
        pl.semaphore_wait(up.at[1], 1)
        row_copy(1).start()
        corner_copy(1).start()
        tell_lower(over_up)

    if n_t > 1:
        put_tail_cols(tail1, tailc1)

        def tails_first(k):
            pl.semaphore_wait(over.at[k], 1)
            for i in (8, 0, 1):
                far(k, me_t, i).start()
            aside(lambda i: far(k, me_t, i).start(), 0)

            @pl.when(has[1])
            def _():
                pl.semaphore_wait(over_up.at[k], 1)

            aside(lambda i: far(k, me_t, i).start(), 1)

        later(tails_first)
    col_copy(True).wait_recv()
    for y in range(R):
        sides(y + 2, as_groups(rows1, y), col_in1[y + 2].astype(f32))
    for c in load_w1:
        c.wait()
    half = (R - 2) // 2
    conv(2, half, wl1, wc1, ws1)
    conv(2 + half, R - 2 - half, wl1, wc1, ws1)
    for side in range(2):
        @pl.when(has[side])
        def _(side=side):
            row_copy(1 - side, -1).wait_recv()
            corner_copy(1 - side, -1).wait_recv()
    for side in range(2):
        for r in range(2):
            v = silu_norm(grouped(raw_in.at[side], (r,)), g1[...].reshape(1, 1, C))
            v = jnp.where(live, v, 0.0)
            yy = side * (R + 2) + r
            v = v.astype(bf16).astype(f32)
            center(yy, v)
            sides(yy, v, col_in1[yy].astype(f32))
    conv(0, 2, wl1, wc1, ws1)
    conv(R, 2, wl1, wc1, ws1)
    if n_t > 1:
        @pl.when(me_t > 0)
        def _():
            before(True, R + 2, wl1, wc1, ws1)

    for c in load_rest:
        c.wait()
    for h in range(R + 2):
        v = silu_norm(acc[pl.ds(h * S, S)] + b1[...], g2[...]).reshape(F, X, C)
        v = jnp.where(live, v, 0.0)
        if h in (0, R + 1):
            v = jnp.where(has[min(h, 1)], v, 0.0)
        rows2[h] = v.reshape(S, C).astype(bf16)
        col_out2[h] = edge(v).astype(bf16)
        if n_t > 1:
            tail2[h] = tail_of(v)
        center(h, v)
    col_copy(False).start()
    if n_t > 1:
        put_tail_cols(tail2, tailc2)


        def tails_second(k):
            for i in (6, 7):
                far(k, me_t, i).start()

        later(tails_second)
    col_copy(False).wait_recv()
    for h in range(R + 2):
        sides(h, as_groups(rows2, h), col_in2[h].astype(f32))
    for c in load_w2:
        c.wait()
    conv(0, R, wl2, wc2, ws2)
    if n_t > 1:
        @pl.when(me_t > 0)
        def _():
            before(False, R, wl2, wc2, ws2)

    for y in range(R):
        result = acc[pl.ds(y * S, S)] + b2[...]
        for g in range(F):
            t = frame_of[g]
            value = feat[t, y].astype(f32) + result[g * X : (g + 1) * X]
            out[t, y] = jnp.where(live[g], value, 0.0).astype(bf16)

    col_copy(True).wait_send()
    col_copy(False).wait_send()
    for side in range(2):
        @pl.when(has[side])
        def _(side=side):
            row_copy(side).wait_send()
            corner_copy(side).wait_send()

    def sent(k):
        for i in (8, 0, 1, 6, 7):
            far(k, me_t, i).wait_send()
        for side in range(2):
            aside(lambda i: far(k, me_t, i).wait_send(), side)

    later(sent)


def shards(sizes, features, frame_counts, gain_first, conv_first, bias_first, gain_second, conv_second, bias_second):
    F, R, X, C = features.shape
    n_t, n_z, n_w = sizes
    assert n_w == 2 and F % 2 == 0 and F >= 4 and X == 8 and 2 * (C - LANES) == LANES and R >= 4
    H = F // 2
    S, T = F * X, 2 * X
    wide = -(-(R + 2) // 16) * 16
    dma = pltpu.SemaphoreType.DMA
    V = pltpu.VMEM
    weights = [V((3, 3, 3, LANES, C), bf16), V((2, 3, LANES, C), bf16), V((3, 3, LANES, C), bf16)]
    scratch = [
        V(features.shape, bf16),
        V((1, C), f32),
        V((1, C), f32),
        V((1, C), f32),
        V((1, C), f32),
        *weights,
        *weights,
        dma((17,)),
        V((3, R + 4, (H + 2) * T, LANES), bf16),
        V((R + 4, (H + 2) * T, LANES), bf16),
        V((R + 4, (H + 2) * T, LANES), bf16),
        V(((R + 2) * S, C), f32),
        V((3, R + 4, 2 * T, LANES), bf16),
        V((R + 4, T, LANES), bf16),
        V((R + 4, 2 * T, LANES), bf16),
        V((X, C), f32),
        V((n_t, X, C), f32),
        V((R + 4, T, C), f32),
        V((3, 2, max(R, wide), C), f32),
        V((2, F, 2, X, C), bf16),
        V((R, S, C), bf16),
        V((R, F, C), bf16),
        V((R + 4, F, C), bf16),
        V((R, T, C), bf16),
        V((2, R, C), bf16),
        V((n_t, R + 4, T, C), bf16),
        V((n_t, 2, R, C), bf16),
        V((n_t, 2, 2, R, C), bf16),
        V((R + 2, S, C), bf16),
        V((R + 2, F, C), bf16),
        V((R + 2, F, C), bf16),
        V((R + 2, T, C), bf16),
        V((2, wide, C), bf16),
        V((n_t, R + 2, T, C), bf16),
        V((n_t, 2, wide, C), bf16),
        dma((6,)),
        dma((6,)),
        dma((n_t, 9)),
        dma((n_t, 9)),
        pltpu.SemaphoreType.REGULAR((2,)),
        pltpu.SemaphoreType.REGULAR((n_t,)),
        pltpu.SemaphoreType.REGULAR((n_t,)),
    ]
    return pl.pallas_call(
        functools.partial(kernel, sizes),
        out_shape=pltpu.VMEM(features.shape, features.dtype),
        in_specs=[pl.BlockSpec(memory_space=pltpu.SMEM)] + [pl.BlockSpec(memory_space=pltpu.HBM)] * 7,
        out_specs=pl.BlockSpec(memory_space=pltpu.VMEM),
        scratch_shapes=scratch,
        compiler_params=pltpu.CompilerParams(
            collective_id=0, has_side_effects=True, vmem_limit_bytes=58 << 20
        ),
    )(
        frame_counts,
        features,
        gain_first.reshape(1, C),
        conv_first,
        bias_first.reshape(1, C),
        gain_second.reshape(1, C),
        conv_second,
        bias_second.reshape(1, C),
    )


def solution(mesh):
    sizes = (mesh.shape["tchunk"], mesh.shape["ha"], mesh.shape["wa"])
    spec = P(("grp", "tchunk"), "ha", "wa", None)
    return jax.shard_map(
        functools.partial(shards, sizes),
        mesh=mesh,
        in_specs=(spec, P(("grp", "tchunk")), P(), P(), P(), P(), P(), P()),
        out_specs=spec,
        check_vma=False,
    )
```

```python
import functools

import jax
import jax.numpy as jnp
from jax import lax
from jax.experimental import pallas as pl
from jax.experimental.pallas import tpu as pltpu
from jax.sharding import PartitionSpec as P

epsilon = 1e-06
MESH = pl.DeviceIdType.MESH
LANES = 128
f32, bf16 = jnp.float32, jnp.bfloat16


def silu_norm(values, gain):
    inverse = lax.rsqrt(jnp.mean(values * values, axis=-1, keepdims=True) + epsilon)
    return jax.nn.silu(values * inverse * gain)


def kernel(sizes, *refs):
    placed, out, scratch = refs[:8], refs[8], refs[9:]
    n_t, n_z, n_w = sizes
    cnt_ref, feat_hbm, g1_hbm, w1_hbm, b1_hbm, g2_hbm, w2_hbm, b2_hbm = placed
    (feat, g1, b1, g2, b2, wl1, wc1, ws1, wl2, wc2, ws2, lsem, lo1, hc1, hs1, lo2, hc2, hs2, acc,
     clo, chc, chs, cnt_own, cnt_in, carry, carry_col,
     raw_in, rows1, col_out1, col_in1, tail1, tailc1, tail_in1, tailc_in1, tailhc_in,
     rows2, col_out2, col_in2, tail2, tailc2, taile2, tail_in2, tailc_in2, taile_in2,
     nsend, nrecv, fsend, frecv, up, over, over_up) = scratch
    F, R, X, C = feat.shape
    H = F // 2
    S = F * X
    T = 2 * X
    me_t, me_z, me_w = lax.axis_index("tchunk"), lax.axis_index("ha"), lax.axis_index("wa")
    left_core = me_w == 0
    has = (me_z > 0, me_z < n_z - 1)
    frame_of = [(g % 2) * H + g // 2 for g in range(F)]

    def load(i, src, dst):
        return pltpu.make_async_copy(src, dst, lsem.at[i])

    def weight_loads(i, w, wl, wc, ws):
        low, high = pl.ds(0, LANES), pl.ds(LANES, C - LANES)
        top, bottom = pl.ds(0, C - LANES), pl.ds(C - LANES, C - LANES)
        return [
            load(i, w.at[:, :, :, low], wl),
            load(i + 1, w.at[0, :, 1, high], wc.at[0, :, top]),
            load(i + 2, w.at[1, :, 1, high], wc.at[0, :, bottom]),
            load(i + 3, w.at[2, :, 1, high], wc.at[1, :, top]),
            load(i + 4, w.at[:, :, 0, high], ws.at[:, :, top]),
            load(i + 5, w.at[:, :, 2, high], ws.at[:, :, bottom]),
        ]

    load_feat = load(0, feat_hbm, feat)
    load_g1 = load(1, g1_hbm, g1)
    load_rest = [load(2, b1_hbm, b1), load(3, g2_hbm, g2), load(4, b2_hbm, b2)]
    load_w1 = weight_loads(5, w1_hbm, wl1, wc1, ws1)
    load_w2 = weight_loads(11, w2_hbm, wl2, wc2, ws2)
    load_feat.start()
    load_g1.start()

    def device(k, dz, flip):
        return {
            "tchunk": k,
            "ha": lax.rem(me_z + dz + n_z, n_z),
            "wa": 1 - me_w if flip else me_w,
        }

    barrier = pltpu.get_barrier_semaphore()

    def greet(k, dz, flip):
        pl.semaphore_signal(barrier, inc=1, device_id=device(k, dz, flip), device_id_type=MESH)

    greet(me_t, 0, True)

    @pl.when(has[1])
    def _():
        greet(me_t, 1, False)
        greet(me_t, 1, True)

    for k in range(1, n_t):
        @pl.when(me_t < k)
        def _(k=k):
            greet(k, 0, False)

    expected = 1 + 2 * has[0].astype(jnp.int32) + me_t

    def tell(sem, k, dz, flip):
        pl.semaphore_signal(sem, inc=1, device_id=device(k, dz, flip), device_id_type=MESH)

    def tell_lower(sems):
        for k in range(1, n_t):
            @pl.when(me_t == k)
            def _(k=k):
                for lower in range(k):
                    tell(sems.at[k], lower, 0, False)

    for c in load_w1 + load_rest + load_w2:
        c.start()

    def remote(src, dst, ssem, rsem, to):
        return pltpu.make_async_remote_copy(src, dst, ssem, rsem, device_id=to, device_id_type=MESH)

    def row_copy(side, way=1):
        src = feat_hbm.at[:, pl.ds((R - 2) * side, 2)]
        return remote(src, raw_in.at[1 - side], nsend.at[side], nrecv.at[side], device(me_t, way * (2 * side - 1), False))

    def corner_copy(side, way=1):
        src = col_out1.at[pl.ds((R - 2) * side, 2)]
        dst = col_in1.at[pl.ds(0 if side else R + 2, 2)]
        i = 2 + side
        return remote(src, dst, nsend.at[i], nrecv.at[i], device(me_t, way * (2 * side - 1), True))

    def col_copy(first):
        src, dst, i = (col_out1, col_in1.at[pl.ds(2, R)], 4) if first else (col_out2, col_in2, 5)
        return remote(src, dst, nsend.at[i], nrecv.at[i], device(me_t, 0, True))

    def far(k, slot, i, way=1):
        src, dst, dz, flip = (
            (tail1, tail_in1.at[slot, pl.ds(0, R)], 0, False),
            (tailc1, tailc_in1.at[slot], 0, True),
            (tail1.at[pl.ds(0, 2)], tail_in1.at[slot, pl.ds(R + 2, 2)], -1, False),
            (tailc1, tailhc_in.at[slot, 1], -1, True),
            (tail1.at[pl.ds(R - 2, 2)], tail_in1.at[slot, pl.ds(R, 2)], 1, False),
            (tailc1, tailhc_in.at[slot, 0], 1, True),
            (tail2.at[pl.ds(0, R - 2)], tail_in2.at[slot, pl.ds(0, R - 2)], 0, False),
            (tailc2, tailc_in2.at[slot], 0, True),
            (cnt_own, cnt_in.at[slot], 0, False),
            (tail2.at[pl.ds(R - 2, 4)], tail_in2.at[slot, pl.ds(R - 2, 4)], 0, False),
            (taile2, taile_in2.at[slot], 0, True),
        )[i]
        return remote(src, dst, fsend.at[k, i], frecv.at[slot, i], device(k, way * dz, flip))

    def later(act):
        for k in range(1, n_t):
            @pl.when(me_t < k)
            def _(k=k):
                act(k)

    def aside(act, side):
        @pl.when(has[side])
        def _():
            for i in (2, 3) if side == 0 else (4, 5):
                act(i)

    for side in range(2):
        @pl.when(jnp.logical_not(has[side]))
        def _(side=side):
            raw_in[side] = jnp.zeros((F, 2, X, C), bf16)
            col_in1[pl.ds(side * (R + 2), 2)] = jnp.zeros((2, F, C), bf16)
            for k in range(n_t - 1):
                tail_in1[k, pl.ds(R + 2 * side, 2)] = jnp.zeros((2, T, C), bf16)
                tailhc_in[k, side] = jnp.zeros((2, R, C), bf16)
    for wc in (wc1, wc2):
        wc[1, :, C - LANES :] = jnp.zeros((3, C - LANES, C), bf16)

    count = cnt_ref[0]
    cnt_own[...] = jnp.full(cnt_own.shape, count.astype(f32), f32)
    group = lax.broadcasted_iota(jnp.int32, (F, X, C), 0)
    live = lax.rem(group, 2) * H + group // 2 < count

    def edge(v, at=0):
        return jnp.where(left_core, v[:, at + X - 1, :], v[:, at, :])

    def tail_of(v):
        got = []
        for f in range(2):
            t = jnp.zeros((X, C), f32)
            for g in range(F):
                t = jnp.where(count - 2 + f == frame_of[g], v[g], t)
            got.append(t)
        return jnp.concatenate(got, axis=0).astype(bf16)

    def slot_of(h):
        return h - 2 if 2 <= h < R else R - 2 + h if h < 2 else h

    def put_tail_cols(tails, dst):
        v = tails[...].astype(f32)
        more = dst.shape[1] - v.shape[0]
        for f in range(2):
            c = edge(v, f * X)
            if more:
                c = jnp.concatenate([c, jnp.zeros((more, C), f32)], axis=0)
            dst[f] = c.astype(bf16)

    def tiles(b):
        zero = jnp.zeros((X, C), f32)
        front = jnp.concatenate([zero, b[2 * (H - 2)], zero, b[2 * (H - 1)]], axis=0)
        return jnp.concatenate([front, b.reshape(S, C)], axis=0).astype(bf16)

    tiles1, tiles2 = (lo1, hc1, hs1), (lo2, hc2, hs2)

    def center(into, yy, v):
        lo, hc, _ = into
        t = tiles(v)
        lo[1, yy] = t[:, :LANES]
        high = t[:, LANES:]
        after = jnp.concatenate([high[T:], jnp.zeros((T, C - LANES), bf16)], axis=0)
        hc[yy] = jnp.concatenate([high, after], axis=1)

    def beside(v, col):
        index = lax.broadcasted_iota(jnp.int32, v.shape, 1)
        none = jnp.zeros(col.shape, f32)
        lcol = jnp.where(left_core, none, col)
        rcol = jnp.where(left_core, col, none)
        left = jnp.where(index == 0, jnp.broadcast_to(lcol[:, None, :], v.shape), pltpu.roll(v, 1, 1))
        right = jnp.where(index == X - 1, jnp.broadcast_to(rcol[:, None, :], v.shape), pltpu.roll(v, X - 1, 1))
        return left, right

    def sides(into, yy, v, col):
        lo, _, hs = into
        left, right = beside(v, col)
        tl, tr = tiles(left), tiles(right)
        lo[0, yy] = tl[:, :LANES]
        lo[2, yy] = tr[:, :LANES]
        hs[yy] = jnp.concatenate([tl[:, LANES:], tr[:, LANES:]], axis=1)

    def grouped(ref, index):
        return jnp.concatenate([ref[(t,) + index].astype(f32)[None] for t in frame_of], axis=0)

    def as_groups(ref, y):
        return ref[y].astype(f32).reshape(F, X, C)

    def conv(of, y0, n, wl, wc, ws, part=None):
        lo, hc, hs = of

        def take(ref, i, a):
            return ref[pl.ds(y0 + i, n), pl.ds(a * T, S)].reshape(n * S, LANES)

        lhs, rhs = [], []
        for i in range(3):
            if part != "sides":
                lhs += [take(lo.at[1], i, a) for a in range(3)] + [take(hc, i, 0), take(hc, i, 2)]
                rhs += [wl[a, i, 1] for a in range(3)] + [wc[0, i], wc[1, i]]
            if part != "center":
                lhs += [take(lo.at[j], i, a) for a in range(3) for j in (0, 2)] + [take(hs, i, a) for a in range(3)]
                rhs += [wl[a, i, j] for a in range(3) for j in (0, 2)] + [ws[a, i] for a in range(3)]
        got = jnp.dot(jnp.concatenate(lhs, axis=1), jnp.concatenate(rhs, axis=0), preferred_element_type=f32)
        if part == "sides":
            acc[pl.ds(y0 * S, n * S)] += got
        else:
            acc[pl.ds(y0 * S, n * S)] = got

    def before(first, n, wl, wc, ws):
        carry[...] = jnp.zeros(carry.shape, f32)
        carry_col[...] = jnp.zeros(carry_col.shape, f32)
        for k in range(n_t - 1):
            @pl.when(me_t > k)
            def _(k=k):
                for i in (8, 0, 1) if first else (6, 7, 9, 10):
                    far(k, k, i).wait_recv()
                if first:
                    @pl.when(has[0])
                    def _():
                        for i in (4, 5):
                            far(k, k, i, -1).wait_recv()

                    @pl.when(has[1])
                    def _():
                        for i in (2, 3):
                            far(k, k, i, -1).wait_recv()

                total = cnt_in[k]

                def merge(total, early0, early1, late0, late1):
                    both, some = total > 1.5, total > 0.5
                    return (
                        jnp.where(both, late0, jnp.where(some, early1, early0)),
                        jnp.where(some, late1, early1),
                    )

                for at in range(n + 2):
                    late = (tail_in1 if first else tail_in2)[k, at].astype(f32)
                    got = merge(total, carry[at, :X], carry[at, X:], late[:X], late[X:])
                    carry[at] = jnp.concatenate(got, axis=0)
                cols = (tailc_in1.at[k], tailhc_in.at[k, 0], tailhc_in.at[k, 1]) if first else (tailc_in2.at[k], taile_in2.at[k])
                for d, ref in enumerate(cols):
                    late = ref[...].astype(f32)
                    there = pl.ds(0, late.shape[1])
                    got = merge(total[:1], carry_col[d, 0, there], carry_col[d, 1, there], late[0], late[1])
                    carry_col[d, 0, there] = got[0]
                    carry_col[d, 1, there] = got[1]

        zero = jnp.zeros((X, C), f32)
        for yy in range(n + 2):
            at = slot_of(yy)
            d, y = (0, at) if at < R - 2 else (1, at - R + 2)
            if first:
                if yy < 2:
                    at, d, y = R + yy, 1, R - 2 + yy
                elif yy < R + 2:
                    at, d, y = yy - 2, 0, yy - 2
                else:
                    d, y = 2, yy - R - 2
            col = jnp.concatenate([carry_col[d, f, y : y + 1] for f in range(2)], axis=0)
            v = carry[at].reshape(2, X, C)
            left, right = beside(v, col)
            made = []
            for j, b in enumerate((left, v, right)):
                t = jnp.concatenate([b[0], b[1], b[1], zero], axis=0).astype(bf16)
                clo[j, yy] = t[:, :LANES]
                made.append(t[:, LANES:])
            chs[yy] = jnp.concatenate([made[0], made[2]], axis=1)
            chc[yy] = jnp.concatenate([made[1][:T], made[1][T:]], axis=1)
        lhs, rhs = [], []
        for i in range(3):
            for a in range(2):
                for j in range(3):
                    lhs.append(clo[j, pl.ds(i, n), pl.ds(a * T, T)].reshape(n * T, LANES))
                lhs.append(chs[pl.ds(i, n), pl.ds(a * T, T)].reshape(n * T, LANES))
                rhs += [wl[a, i].reshape(3 * LANES, C), ws[a, i]]
            lhs.append(chc[pl.ds(i, n)].reshape(n * T, LANES))
            rhs.append(wc[0, i])
        part = jnp.dot(jnp.concatenate(lhs, axis=1), jnp.concatenate(rhs, axis=0), preferred_element_type=f32)
        for y in range(n):
            for f in range(2):
                acc[pl.ds(y * S + f * T, X)] += part[y * T + f * X : y * T + (f + 1) * X]

    pl.semaphore_wait(barrier, expected)
    tell_lower(over)

    @pl.when(has[0])
    def _():
        tell(up.at[0], me_t, -1, False)
        tell(up.at[1], me_t, -1, True)
        row_copy(0).start()

    load_feat.wait()
    load_g1.wait()

    def keep_first(y):
        v = silu_norm(grouped(feat, (y,)), g1[...].reshape(1, 1, C))
        v = jnp.where(live, v, 0.0)
        rows1[y] = v.reshape(S, C).astype(bf16)
        col_out1[y] = edge(v).astype(bf16)
        if n_t > 1:
            tail1[y] = tail_of(v)
        center(tiles1, y + 2, v)

    ends = sorted({0, 1, R - 2, R - 1})
    for y in ends:
        keep_first(y)

    @pl.when(has[0])
    def _():
        corner_copy(0).start()

    for y in range(R):
        if y not in ends:
            keep_first(y)
    col_copy(True).start()

    @pl.when(has[1])
    def _():
        pl.semaphore_wait(up.at[0], 1)
        pl.semaphore_wait(up.at[1], 1)
        row_copy(1).start()
        corner_copy(1).start()
        tell_lower(over_up)

    if n_t > 1:
        put_tail_cols(tail1, tailc1)

        def tails_first(k):
            pl.semaphore_wait(over.at[k], 1)
            for i in (8, 0, 1):
                far(k, me_t, i).start()
            aside(lambda i: far(k, me_t, i).start(), 0)

            @pl.when(has[1])
            def _():
                pl.semaphore_wait(over_up.at[k], 1)

            aside(lambda i: far(k, me_t, i).start(), 1)

        later(tails_first)
    col_copy(True).wait_recv()
    for y in range(R):
        sides(tiles1, y + 2, as_groups(rows1, y), col_in1[y + 2].astype(f32))
    for c in load_w1:
        c.wait()
    half = (R - 2) // 2
    conv(tiles1, 2, half, wl1, wc1, ws1)
    conv(tiles1, 2 + half, R - 2 - half, wl1, wc1, ws1)
    for c in load_rest:
        c.wait()

    def second(h, groups):
        v = silu_norm(acc[pl.ds(h * S, groups * X)] + b1[...], g2[...]).reshape(groups, X, C)
        v = jnp.where(live[:groups], v, 0.0)
        if h in (0, R + 1):
            v = jnp.where(has[min(h, 1)], v, 0.0)
        rows2[h, : groups * X] = v.reshape(groups * X, C).astype(bf16)
        return v

    def keep_second(h, v, tails=n_t > 1):
        if tails:
            tail2[slot_of(h)] = tail_of(v)
        col_out2[h] = edge(v).astype(bf16)
        center(tiles2, h, v)

    def tails_second(which):
        def act(k):
            for i in which:
                far(k, me_t, i).start()

        return act

    for h in range(2, R):
        keep_second(h, second(h, F))
    if n_t > 1:
        @pl.when(me_t == 0)
        def _():
            put_tail_cols(tail2.at[pl.ds(0, R - 2)], tailc2)
            later(tails_second((6, 7)))

    for side in range(2):
        @pl.when(has[side])
        def _(side=side):
            row_copy(1 - side, -1).wait_recv()
            corner_copy(1 - side, -1).wait_recv()
    for side in range(2):
        for r in range(2):
            v = silu_norm(grouped(raw_in.at[side], (r,)), g1[...].reshape(1, 1, C))
            v = jnp.where(live, v, 0.0)
            yy = side * (R + 2) + r
            v = v.astype(bf16).astype(f32)
            center(tiles1, yy, v)
            sides(tiles1, yy, v, col_in1[yy].astype(f32))
    conv(tiles1, 0, 2, wl1, wc1, ws1)
    conv(tiles1, R, 2, wl1, wc1, ws1)
    for h in (0, 1, R, R + 1):
        keep_second(h, second(h, F))
    if n_t > 1:
        @pl.when(me_t == 0)
        def _():
            put_tail_cols(tail2.at[pl.ds(R - 2, 4)], taile2)
            later(tails_second((9, 10)))

        @pl.when(me_t > 0)
        def _():
            before(True, R + 2, wl1, wc1, ws1)
            for h in range(R + 2):
                v = second(h, 4)
                rest = rows2[h, 4 * X :].astype(f32).reshape(F - 4, X, C)
                keep_second(h, jnp.concatenate([v, rest], axis=0), n_t > 2)
            if n_t > 2:
                put_tail_cols(tail2.at[pl.ds(0, R - 2)], tailc2)
                put_tail_cols(tail2.at[pl.ds(R - 2, 4)], taile2)
                later(tails_second((6, 7, 9, 10)))

    col_copy(False).start()

    for c in load_w2:
        c.wait()
    for y in (0, R // 2):
        conv(tiles2, y, R // 2 if y == 0 else R - R // 2, wl2, wc2, ws2, "center")
    col_copy(False).wait_recv()
    for h in range(R + 2):
        sides(tiles2, h, as_groups(rows2, h), col_in2[h].astype(f32))
    for y in (0, R // 2):
        conv(tiles2, y, R // 2 if y == 0 else R - R // 2, wl2, wc2, ws2, "sides")
    if n_t > 1:
        @pl.when(me_t > 0)
        def _():
            before(False, R, wl2, wc2, ws2)

    for y in range(R):
        result = acc[pl.ds(y * S, S)] + b2[...]
        for g in range(F):
            t = frame_of[g]
            value = feat[t, y].astype(f32) + result[g * X : (g + 1) * X]
            out[t, y] = jnp.where(live[g], value, 0.0).astype(bf16)

    col_copy(True).wait_send()
    col_copy(False).wait_send()
    for side in range(2):
        @pl.when(has[side])
        def _(side=side):
            row_copy(side).wait_send()
            corner_copy(side).wait_send()

    def sent(k):
        for i in (8, 0, 1, 6, 7, 9, 10):
            far(k, me_t, i).wait_send()
        for side in range(2):
            aside(lambda i: far(k, me_t, i).wait_send(), side)

    later(sent)


def shards(sizes, features, frame_counts, gain_first, conv_first, bias_first, gain_second, conv_second, bias_second):
    F, R, X, C = features.shape
    n_t, n_z, n_w = sizes
    assert n_w == 2 and F % 2 == 0 and F >= 4 and X == 8 and 2 * (C - LANES) == LANES and R >= 4
    H = F // 2
    S, T = F * X, 2 * X
    inner = -(-(R - 2) // 8) * 8
    dma = pltpu.SemaphoreType.DMA
    V = pltpu.VMEM
    weights = [V((3, 3, 3, LANES, C), bf16), V((2, 3, LANES, C), bf16), V((3, 3, LANES, C), bf16)]
    scratch = [
        V(features.shape, bf16),
        V((1, C), f32),
        V((1, C), f32),
        V((1, C), f32),
        V((1, C), f32),
        *weights,
        *weights,
        dma((17,)),
        V((3, R + 4, (H + 2) * T, LANES), bf16),
        V((R + 4, (H + 2) * T, LANES), bf16),
        V((R + 4, (H + 2) * T, LANES), bf16),
        V((3, R + 2, (H + 2) * T, LANES), bf16),
        V((R + 2, (H + 2) * T, LANES), bf16),
        V((R + 2, (H + 2) * T, LANES), bf16),
        V(((R + 2) * S, C), f32),
        V((3, R + 4, 2 * T, LANES), bf16),
        V((R + 4, T, LANES), bf16),
        V((R + 4, 2 * T, LANES), bf16),
        V((X, C), f32),
        V((n_t, X, C), f32),
        V((R + 4, T, C), f32),
        V((3, 2, max(R, inner, 8), C), f32),
        V((2, F, 2, X, C), bf16),
        V((R, S, C), bf16),
        V((R, F, C), bf16),
        V((R + 4, F, C), bf16),
        V((R, T, C), bf16),
        V((2, R, C), bf16),
        V((n_t, R + 4, T, C), bf16),
        V((n_t, 2, R, C), bf16),
        V((n_t, 2, 2, R, C), bf16),
        V((R + 2, S, C), bf16),
        V((R + 2, F, C), bf16),
        V((R + 2, F, C), bf16),
        V((R + 2, T, C), bf16),
        V((2, inner, C), bf16),
        V((2, 8, C), bf16),
        V((n_t, R + 2, T, C), bf16),
        V((n_t, 2, inner, C), bf16),
        V((n_t, 2, 8, C), bf16),
        dma((6,)),
        dma((6,)),
        dma((n_t, 11)),
        dma((n_t, 11)),
        pltpu.SemaphoreType.REGULAR((2,)),
        pltpu.SemaphoreType.REGULAR((n_t,)),
        pltpu.SemaphoreType.REGULAR((n_t,)),
    ]
    return pl.pallas_call(
        functools.partial(kernel, sizes),
        out_shape=pltpu.VMEM(features.shape, features.dtype),
        in_specs=[pl.BlockSpec(memory_space=pltpu.SMEM)] + [pl.BlockSpec(memory_space=pltpu.HBM)] * 7,
        out_specs=pl.BlockSpec(memory_space=pltpu.VMEM),
        scratch_shapes=scratch,
        compiler_params=pltpu.CompilerParams(
            collective_id=0, has_side_effects=True, vmem_limit_bytes=58 << 20
        ),
    )(
        frame_counts,
        features,
        gain_first.reshape(1, C),
        conv_first,
        bias_first.reshape(1, C),
        gain_second.reshape(1, C),
        conv_second,
        bias_second.reshape(1, C),
    )


def solution(mesh):
    sizes = (mesh.shape["tchunk"], mesh.shape["ha"], mesh.shape["wa"])
    spec = P(("grp", "tchunk"), "ha", "wa", None)
    return jax.shard_map(
        functools.partial(shards, sizes),
        mesh=mesh,
        in_specs=(spec, P(("grp", "tchunk")), P(), P(), P(), P(), P(), P()),
        out_specs=spec,
        check_vma=False,
    )
```

```python
import functools

import jax
import jax.numpy as jnp
from jax import lax
from jax.experimental import pallas as pl
from jax.experimental.pallas import tpu as pltpu
from jax.sharding import PartitionSpec as P

epsilon = 1e-06
MESH = pl.DeviceIdType.MESH
LANES = 128
f32, bf16 = jnp.float32, jnp.bfloat16


def silu_norm(values, gain):
    inverse = lax.rsqrt(jnp.mean(values * values, axis=-1, keepdims=True) + epsilon)
    return jax.nn.silu(values * inverse * gain)


def kernel(sizes, *refs):
    placed, out, scratch = refs[:8], refs[8], refs[9:]
    n_t, n_z, n_w = sizes
    cnt_ref, feat_hbm, g1_hbm, w1_hbm, b1_hbm, g2_hbm, w2_hbm, b2_hbm = placed
    (feat, g1, b1, g2, b2, wl1, wc1, ws1, wl2, wc2, ws2, lsem, lo1, hc1, hs1, lo2, hc2, hs2, acc,
     clo, chc, chs, cnt_own, cnt_in, carry, carry_col,
     raw_in, rows1, col_out1, col_in1, tail1, tailc1, tail_in1, tailc_in1, tailhc_in,
     rows2, col_out2, col_in2, tail2, tailc2, taile2, tail_in2, tailc_in2, taile_in2,
     nsend, nrecv, fsend, frecv, up, over, over_up) = scratch
    F, R, X, C = feat.shape
    H = F // 2
    S = F * X
    T = 2 * X
    me_t, me_z, me_w = lax.axis_index("tchunk"), lax.axis_index("ha"), lax.axis_index("wa")
    left_core = me_w == 0
    has = (me_z > 0, me_z < n_z - 1)
    frame_of = [(g % 2) * H + g // 2 for g in range(F)]

    def load(i, src, dst):
        return pltpu.make_async_copy(src, dst, lsem.at[i])

    def weight_loads(i, w, wl, wc, ws):
        low, high = pl.ds(0, LANES), pl.ds(LANES, C - LANES)
        top, bottom = pl.ds(0, C - LANES), pl.ds(C - LANES, C - LANES)
        return [
            load(i, w.at[:, :, :, low], wl),
            load(i + 1, w.at[0, :, 1, high], wc.at[0, :, top]),
            load(i + 2, w.at[1, :, 1, high], wc.at[0, :, bottom]),
            load(i + 3, w.at[2, :, 1, high], wc.at[1, :, top]),
            load(i + 4, w.at[:, :, 0, high], ws.at[:, :, top]),
            load(i + 5, w.at[:, :, 2, high], ws.at[:, :, bottom]),
        ]

    load_feat = load(0, feat_hbm, feat)
    load_g1 = load(1, g1_hbm, g1)
    load_rest = [load(2, b1_hbm, b1), load(3, g2_hbm, g2), load(4, b2_hbm, b2)]
    load_w1 = weight_loads(5, w1_hbm, wl1, wc1, ws1)
    load_w2 = weight_loads(11, w2_hbm, wl2, wc2, ws2)
    load_feat.start()
    load_g1.start()

    def device(k, dz, flip):
        return {
            "tchunk": k,
            "ha": lax.rem(me_z + dz + n_z, n_z),
            "wa": 1 - me_w if flip else me_w,
        }

    barrier = pltpu.get_barrier_semaphore()

    def greet(k, dz, flip):
        pl.semaphore_signal(barrier, inc=1, device_id=device(k, dz, flip), device_id_type=MESH)

    greet(me_t, 0, True)

    @pl.when(has[1])
    def _():
        greet(me_t, 1, False)
        greet(me_t, 1, True)

    for k in range(1, n_t):
        @pl.when(me_t < k)
        def _(k=k):
            greet(k, 0, False)

    expected = 1 + 2 * has[0].astype(jnp.int32) + me_t

    def tell(sem, k, dz, flip):
        pl.semaphore_signal(sem, inc=1, device_id=device(k, dz, flip), device_id_type=MESH)

    def tell_lower(sems):
        for k in range(1, n_t):
            @pl.when(me_t == k)
            def _(k=k):
                for lower in range(k):
                    tell(sems.at[k], lower, 0, False)

    for c in load_w1 + load_rest + load_w2:
        c.start()

    def remote(src, dst, ssem, rsem, to):
        return pltpu.make_async_remote_copy(src, dst, ssem, rsem, device_id=to, device_id_type=MESH)

    def row_copy(side, way=1):
        src = feat_hbm.at[:, pl.ds((R - 2) * side, 2)]
        return remote(src, raw_in.at[1 - side], nsend.at[side], nrecv.at[side], device(me_t, way * (2 * side - 1), False))

    def corner_copy(side, way=1):
        src = col_out1.at[pl.ds((R - 2) * side, 2)]
        dst = col_in1.at[pl.ds(0 if side else R + 2, 2)]
        i = 2 + side
        return remote(src, dst, nsend.at[i], nrecv.at[i], device(me_t, way * (2 * side - 1), True))

    def col_copy(first):
        src, dst, i = (col_out1, col_in1.at[pl.ds(2, R)], 4) if first else (col_out2, col_in2, 5)
        return remote(src, dst, nsend.at[i], nrecv.at[i], device(me_t, 0, True))

    def far(k, slot, i, way=1):
        src, dst, dz, flip = (
            (tail1, tail_in1.at[slot, pl.ds(0, R)], 0, False),
            (tailc1, tailc_in1.at[slot], 0, True),
            (tail1.at[pl.ds(0, 2)], tail_in1.at[slot, pl.ds(R + 2, 2)], -1, False),
            (tailc1, tailhc_in.at[slot, 1], -1, True),
            (tail1.at[pl.ds(R - 2, 2)], tail_in1.at[slot, pl.ds(R, 2)], 1, False),
            (tailc1, tailhc_in.at[slot, 0], 1, True),
            (tail2.at[pl.ds(0, R - 2)], tail_in2.at[slot, pl.ds(0, R - 2)], 0, False),
            (tailc2, tailc_in2.at[slot], 0, True),
            (cnt_own, cnt_in.at[slot], 0, False),
            (tail2.at[pl.ds(R - 2, 4)], tail_in2.at[slot, pl.ds(R - 2, 4)], 0, False),
            (taile2, taile_in2.at[slot], 0, True),
        )[i]
        return remote(src, dst, fsend.at[k, i], frecv.at[slot, i], device(k, way * dz, flip))

    def later(act):
        for k in range(1, n_t):
            @pl.when(me_t < k)
            def _(k=k):
                act(k)

    def aside(act, side):
        @pl.when(has[side])
        def _():
            for i in (2, 3) if side == 0 else (4, 5):
                act(i)

    for side in range(2):
        @pl.when(jnp.logical_not(has[side]))
        def _(side=side):
            raw_in[side] = jnp.zeros((F, 2, X, C), bf16)
            col_in1[pl.ds(side * (R + 2), 2)] = jnp.zeros((2, F, C), bf16)
            for k in range(n_t - 1):
                tail_in1[k, pl.ds(R + 2 * side, 2)] = jnp.zeros((2, T, C), bf16)
                tailhc_in[k, side] = jnp.zeros((2, R, C), bf16)
    for wc in (wc1, wc2):
        wc[1, :, C - LANES :] = jnp.zeros((3, C - LANES, C), bf16)

    count = cnt_ref[0]
    cnt_own[...] = jnp.full(cnt_own.shape, count.astype(f32), f32)
    group = lax.broadcasted_iota(jnp.int32, (F, X, C), 0)
    live = lax.rem(group, 2) * H + group // 2 < count

    def edge(v, at=0):
        return jnp.where(left_core, v[:, at + X - 1, :], v[:, at, :])

    def tail_of(v):
        got = []
        for f in range(2):
            t = jnp.zeros((X, C), f32)
            for g in range(F):
                t = jnp.where(count - 2 + f == frame_of[g], v[g], t)
            got.append(t)
        return jnp.concatenate(got, axis=0).astype(bf16)

    def slot_of(h):
        return h - 2 if 2 <= h < R else R - 2 + h if h < 2 else h

    def put_tail_cols(tails, dst):
        v = tails[...].astype(f32)
        more = dst.shape[1] - v.shape[0]
        for f in range(2):
            c = edge(v, f * X)
            if more:
                c = jnp.concatenate([c, jnp.zeros((more, C), f32)], axis=0)
            dst[f] = c.astype(bf16)

    def tiles(b):
        zero = jnp.zeros((X, C), f32)
        front = jnp.concatenate([zero, b[2 * (H - 2)], zero, b[2 * (H - 1)]], axis=0)
        return jnp.concatenate([front, b.reshape(S, C)], axis=0).astype(bf16)

    tiles1, tiles2 = (lo1, hc1, hs1), (lo2, hc2, hs2)

    def center(into, yy, v):
        lo, hc, _ = into
        t = tiles(v)
        lo[1, yy] = t[:, :LANES]
        high = t[:, LANES:]
        after = jnp.concatenate([high[T:], jnp.zeros((T, C - LANES), bf16)], axis=0)
        hc[yy] = jnp.concatenate([high, after], axis=1)

    def beside(v, col):
        index = lax.broadcasted_iota(jnp.int32, v.shape, 1)
        none = jnp.zeros(col.shape, f32)
        lcol = jnp.where(left_core, none, col)
        rcol = jnp.where(left_core, col, none)
        left = jnp.where(index == 0, jnp.broadcast_to(lcol[:, None, :], v.shape), pltpu.roll(v, 1, 1))
        right = jnp.where(index == X - 1, jnp.broadcast_to(rcol[:, None, :], v.shape), pltpu.roll(v, X - 1, 1))
        return left, right

    def sides(into, yy, v, col):
        lo, _, hs = into
        left, right = beside(v, col)
        tl, tr = tiles(left), tiles(right)
        lo[0, yy] = tl[:, :LANES]
        lo[2, yy] = tr[:, :LANES]
        hs[yy] = jnp.concatenate([tl[:, LANES:], tr[:, LANES:]], axis=1)

    def grouped(ref, index):
        return jnp.concatenate([ref[(t,) + index].astype(f32)[None] for t in frame_of], axis=0)

    def as_groups(ref, y):
        return ref[y].astype(f32).reshape(F, X, C)

    def conv(of, y0, n, wl, wc, ws, part=None, taps=(0, 1, 2), add=False):
        lo, hc, hs = of

        def take(ref, i, a):
            return ref[pl.ds(y0 + i, n), pl.ds(a * T, S)].reshape(n * S, LANES)

        lhs, rhs = [], []
        for i in taps:
            if part != "sides":
                lhs += [take(lo.at[1], i, a) for a in range(3)] + [take(hc, i, 0), take(hc, i, 2)]
                rhs += [wl[a, i, 1] for a in range(3)] + [wc[0, i], wc[1, i]]
            if part != "center":
                lhs += [take(lo.at[j], i, a) for a in range(3) for j in (0, 2)] + [take(hs, i, a) for a in range(3)]
                rhs += [wl[a, i, j] for a in range(3) for j in (0, 2)] + [ws[a, i] for a in range(3)]
        got = jnp.dot(jnp.concatenate(lhs, axis=1), jnp.concatenate(rhs, axis=0), preferred_element_type=f32)
        if part == "sides" or add:
            acc[pl.ds(y0 * S, n * S)] += got
        else:
            acc[pl.ds(y0 * S, n * S)] = got

    def before(first, n, wl, wc, ws):
        carry[...] = jnp.zeros(carry.shape, f32)
        carry_col[...] = jnp.zeros(carry_col.shape, f32)
        for k in range(n_t - 1):
            @pl.when(me_t > k)
            def _(k=k):
                for i in (8, 0, 1) if first else (6, 7, 9, 10):
                    far(k, k, i).wait_recv()
                if first:
                    @pl.when(has[0])
                    def _():
                        for i in (4, 5):
                            far(k, k, i, -1).wait_recv()

                    @pl.when(has[1])
                    def _():
                        for i in (2, 3):
                            far(k, k, i, -1).wait_recv()

                total = cnt_in[k]

                def merge(total, early0, early1, late0, late1):
                    both, some = total > 1.5, total > 0.5
                    return (
                        jnp.where(both, late0, jnp.where(some, early1, early0)),
                        jnp.where(some, late1, early1),
                    )

                for at in range(n + 2):
                    late = (tail_in1 if first else tail_in2)[k, at].astype(f32)
                    got = merge(total, carry[at, :X], carry[at, X:], late[:X], late[X:])
                    carry[at] = jnp.concatenate(got, axis=0)
                cols = (tailc_in1.at[k], tailhc_in.at[k, 0], tailhc_in.at[k, 1]) if first else (tailc_in2.at[k], taile_in2.at[k])
                for d, ref in enumerate(cols):
                    late = ref[...].astype(f32)
                    there = pl.ds(0, late.shape[1])
                    got = merge(total[:1], carry_col[d, 0, there], carry_col[d, 1, there], late[0], late[1])
                    carry_col[d, 0, there] = got[0]
                    carry_col[d, 1, there] = got[1]

        zero = jnp.zeros((X, C), f32)
        for yy in range(n + 2):
            at = slot_of(yy)
            d, y = (0, at) if at < R - 2 else (1, at - R + 2)
            if first:
                if yy < 2:
                    at, d, y = R + yy, 1, R - 2 + yy
                elif yy < R + 2:
                    at, d, y = yy - 2, 0, yy - 2
                else:
                    d, y = 2, yy - R - 2
            col = jnp.concatenate([carry_col[d, f, y : y + 1] for f in range(2)], axis=0)
            v = carry[at].reshape(2, X, C)
            left, right = beside(v, col)
            made = []
            for j, b in enumerate((left, v, right)):
                t = jnp.concatenate([b[0], b[1], b[1], zero], axis=0).astype(bf16)
                clo[j, yy] = t[:, :LANES]
                made.append(t[:, LANES:])
            chs[yy] = jnp.concatenate([made[0], made[2]], axis=1)
            chc[yy] = jnp.concatenate([made[1][:T], made[1][T:]], axis=1)
        lhs, rhs = [], []
        for i in range(3):
            for a in range(2):
                for j in range(3):
                    lhs.append(clo[j, pl.ds(i, n), pl.ds(a * T, T)].reshape(n * T, LANES))
                lhs.append(chs[pl.ds(i, n), pl.ds(a * T, T)].reshape(n * T, LANES))
                rhs += [wl[a, i].reshape(3 * LANES, C), ws[a, i]]
            lhs.append(chc[pl.ds(i, n)].reshape(n * T, LANES))
            rhs.append(wc[0, i])
        part = jnp.dot(jnp.concatenate(lhs, axis=1), jnp.concatenate(rhs, axis=0), preferred_element_type=f32)
        for y in range(n):
            for f in range(2):
                acc[pl.ds(y * S + f * T, X)] += part[y * T + f * X : y * T + (f + 1) * X]

    pl.semaphore_wait(barrier, expected)
    tell_lower(over)

    @pl.when(has[0])
    def _():
        tell(up.at[0], me_t, -1, False)
        tell(up.at[1], me_t, -1, True)
        row_copy(0).start()

    load_feat.wait()
    load_g1.wait()

    def keep_first(y):
        v = silu_norm(grouped(feat, (y,)), g1[...].reshape(1, 1, C))
        v = jnp.where(live, v, 0.0)
        rows1[y] = v.reshape(S, C).astype(bf16)
        col_out1[y] = edge(v).astype(bf16)
        center(tiles1, y + 2, v)

    ends = sorted({0, 1, R - 2, R - 1})
    for y in ends:
        keep_first(y)

    @pl.when(has[0])
    def _():
        corner_copy(0).start()

    for y in range(R):
        if y not in ends:
            keep_first(y)
    col_copy(True).start()

    @pl.when(has[1])
    def _():
        pl.semaphore_wait(up.at[0], 1)
        row_copy(1).start()
        pl.semaphore_wait(up.at[1], 1)
        corner_copy(1).start()
        tell_lower(over_up)

    if n_t > 1:
        @pl.when(me_t < n_t - 1)
        def _():
            for y in range(R):
                tail1[y] = tail_of(as_groups(rows1, y))
            put_tail_cols(tail1, tailc1)

        def tails_first(k):
            pl.semaphore_wait(over.at[k], 1)
            for i in (8, 0, 1):
                far(k, me_t, i).start()
            aside(lambda i: far(k, me_t, i).start(), 0)

        def tails_up(k):
            @pl.when(has[1])
            def _():
                pl.semaphore_wait(over_up.at[k], 1)
                for i in (4, 5):
                    far(k, me_t, i).start()

        later(tails_first)
    col_copy(True).wait_recv()
    for y in range(R):
        sides(tiles1, y + 2, as_groups(rows1, y), col_in1[y + 2].astype(f32))
    if n_t > 1:
        @pl.when(me_z > 0)
        def _():
            later(tails_up)

    for c in load_w1:
        c.wait()
    half = (R - 2) // 2
    conv(tiles1, 2, half, wl1, wc1, ws1)
    conv(tiles1, 2 + half, R - 2 - half, wl1, wc1, ws1)
    conv(tiles1, 0, 2, wl1, wc1, ws1, taps=(2,))
    conv(tiles1, R, 2, wl1, wc1, ws1, taps=(0,))
    if n_t > 1:
        @pl.when(me_z == 0)
        def _():
            later(tails_up)

    for c in load_rest:
        c.wait()

    def second(h, groups):
        v = silu_norm(acc[pl.ds(h * S, groups * X)] + b1[...], g2[...]).reshape(groups, X, C)
        v = jnp.where(live[:groups], v, 0.0)
        if h in (0, R + 1):
            v = jnp.where(has[min(h, 1)], v, 0.0)
        rows2[h, : groups * X] = v.reshape(groups * X, C).astype(bf16)
        return v

    def keep_second(h, v):
        col_out2[h] = edge(v).astype(bf16)
        center(tiles2, h, v)

    def put_tails(rows, at, n, dst):
        for h in rows:
            tail2[slot_of(h)] = tail_of(as_groups(rows2, h))
        put_tail_cols(tail2.at[pl.ds(at, n)], dst)

    def tails_second(which):
        def act(k):
            for i in which:
                far(k, me_t, i).start()

        return act

    for h in range(2, R):
        keep_second(h, second(h, F))
    if n_t > 1:
        @pl.when(me_t == 0)
        def _():
            put_tails(range(2, R), 0, R - 2, tailc2)
            later(tails_second((6, 7)))

    for side in range(2):
        @pl.when(has[side])
        def _(side=side):
            row_copy(1 - side, -1).wait_recv()
            corner_copy(1 - side, -1).wait_recv()
    for side in range(2):
        for r in range(2):
            v = silu_norm(grouped(raw_in.at[side], (r,)), g1[...].reshape(1, 1, C))
            v = jnp.where(live, v, 0.0)
            yy = side * (R + 2) + r
            v = v.astype(bf16).astype(f32)
            center(tiles1, yy, v)
            sides(tiles1, yy, v, col_in1[yy].astype(f32))
    conv(tiles1, 0, 2, wl1, wc1, ws1, taps=(0, 1), add=True)
    conv(tiles1, R, 2, wl1, wc1, ws1, taps=(1, 2), add=True)
    ends = (0, 1, R, R + 1)

    @pl.when(me_t == 0)
    def _():
        for h in ends:
            keep_second(h, second(h, F))
        if n_t > 1:
            put_tails(ends, R - 2, 4, taile2)
            later(tails_second((9, 10)))

    if n_t > 1:
        @pl.when(me_t > 0)
        def _():
            before(True, R + 2, wl1, wc1, ws1)
            for h in ends:
                keep_second(h, second(h, F))
            for h in range(2, R):
                v = second(h, 4)
                rest = rows2[h, 4 * X :].astype(f32).reshape(F - 4, X, C)
                v = jnp.concatenate([v, rest], axis=0)
                col_out2[h] = edge(v).astype(bf16)
                t = jnp.concatenate([jnp.zeros((X, C), f32), v[2 * (H - 1)], v[:6].reshape(6 * X, C)], axis=0)
                t = t.astype(bf16)
                high = t[:, LANES:]
                lo2[1, h, 2 * T : 4 * T] = t[T : 3 * T, :LANES]
                hc2[h, T : 4 * T] = jnp.concatenate([high[: 3 * T], high[T:]], axis=1)
            if n_t > 2:
                @pl.when(me_t < n_t - 1)
                def _():
                    put_tails(range(2, R), 0, R - 2, tailc2)
                    put_tails(ends, R - 2, 4, taile2)
                    later(tails_second((6, 7, 9, 10)))

    col_copy(False).start()

    for c in load_w2:
        c.wait()
    for y in (0, R // 2):
        conv(tiles2, y, R // 2 if y == 0 else R - R // 2, wl2, wc2, ws2, "center")
    col_copy(False).wait_recv()
    for h in range(R + 2):
        sides(tiles2, h, as_groups(rows2, h), col_in2[h].astype(f32))
    for y in (0, R // 2):
        conv(tiles2, y, R // 2 if y == 0 else R - R // 2, wl2, wc2, ws2, "sides")
    if n_t > 1:
        @pl.when(me_t > 0)
        def _():
            before(False, R, wl2, wc2, ws2)

    for y in range(R):
        result = acc[pl.ds(y * S, S)] + b2[...]
        for g in range(F):
            t = frame_of[g]
            value = feat[t, y].astype(f32) + result[g * X : (g + 1) * X]
            out[t, y] = jnp.where(live[g], value, 0.0).astype(bf16)

    col_copy(True).wait_send()
    col_copy(False).wait_send()
    for side in range(2):
        @pl.when(has[side])
        def _(side=side):
            row_copy(side).wait_send()
            corner_copy(side).wait_send()

    def sent(k):
        for i in (8, 0, 1, 6, 7, 9, 10):
            far(k, me_t, i).wait_send()
        for side in range(2):
            aside(lambda i: far(k, me_t, i).wait_send(), side)

    later(sent)


def shards(sizes, features, frame_counts, gain_first, conv_first, bias_first, gain_second, conv_second, bias_second):
    F, R, X, C = features.shape
    n_t, n_z, n_w = sizes
    assert n_w == 2 and F % 2 == 0 and F >= 6 and X == 8 and 2 * (C - LANES) == LANES and R >= 4
    H = F // 2
    S, T = F * X, 2 * X
    inner = -(-(R - 2) // 8) * 8
    dma = pltpu.SemaphoreType.DMA
    V = pltpu.VMEM
    weights = [V((3, 3, 3, LANES, C), bf16), V((2, 3, LANES, C), bf16), V((3, 3, LANES, C), bf16)]
    scratch = [
        V(features.shape, bf16),
        V((1, C), f32),
        V((1, C), f32),
        V((1, C), f32),
        V((1, C), f32),
        *weights,
        *weights,
        dma((17,)),
        V((3, R + 4, (H + 2) * T, LANES), bf16),
        V((R + 4, (H + 2) * T, LANES), bf16),
        V((R + 4, (H + 2) * T, LANES), bf16),
        V((3, R + 2, (H + 2) * T, LANES), bf16),
        V((R + 2, (H + 2) * T, LANES), bf16),
        V((R + 2, (H + 2) * T, LANES), bf16),
        V(((R + 2) * S, C), f32),
        V((3, R + 4, 2 * T, LANES), bf16),
        V((R + 4, T, LANES), bf16),
        V((R + 4, 2 * T, LANES), bf16),
        V((X, C), f32),
        V((n_t, X, C), f32),
        V((R + 4, T, C), f32),
        V((3, 2, max(R, inner, 8), C), f32),
        V((2, F, 2, X, C), bf16),
        V((R, S, C), bf16),
        V((R, F, C), bf16),
        V((R + 4, F, C), bf16),
        V((R, T, C), bf16),
        V((2, R, C), bf16),
        V((n_t, R + 4, T, C), bf16),
        V((n_t, 2, R, C), bf16),
        V((n_t, 2, 2, R, C), bf16),
        V((R + 2, S, C), bf16),
        V((R + 2, F, C), bf16),
        V((R + 2, F, C), bf16),
        V((R + 2, T, C), bf16),
        V((2, inner, C), bf16),
        V((2, 8, C), bf16),
        V((n_t, R + 2, T, C), bf16),
        V((n_t, 2, inner, C), bf16),
        V((n_t, 2, 8, C), bf16),
        dma((6,)),
        dma((6,)),
        dma((n_t, 11)),
        dma((n_t, 11)),
        pltpu.SemaphoreType.REGULAR((2,)),
        pltpu.SemaphoreType.REGULAR((n_t,)),
        pltpu.SemaphoreType.REGULAR((n_t,)),
    ]
    return pl.pallas_call(
        functools.partial(kernel, sizes),
        out_shape=pltpu.VMEM(features.shape, features.dtype),
        in_specs=[pl.BlockSpec(memory_space=pltpu.SMEM)] + [pl.BlockSpec(memory_space=pltpu.HBM)] * 7,
        out_specs=pl.BlockSpec(memory_space=pltpu.VMEM),
        scratch_shapes=scratch,
        compiler_params=pltpu.CompilerParams(
            collective_id=0, has_side_effects=True, vmem_limit_bytes=58 << 20
        ),
    )(
        frame_counts,
        features,
        gain_first.reshape(1, C),
        conv_first,
        bias_first.reshape(1, C),
        gain_second.reshape(1, C),
        conv_second,
        bias_second.reshape(1, C),
    )


def solution(mesh):
    sizes = (mesh.shape["tchunk"], mesh.shape["ha"], mesh.shape["wa"])
    spec = P(("grp", "tchunk"), "ha", "wa", None)
    return jax.shard_map(
        functools.partial(shards, sizes),
        mesh=mesh,
        in_specs=(spec, P(("grp", "tchunk")), P(), P(), P(), P(), P(), P()),
        out_specs=spec,
        check_vma=False,
    )
```

```python
import functools

import jax
import jax.numpy as jnp
from jax import lax
from jax.experimental import pallas as pl
from jax.experimental.pallas import tpu as pltpu
from jax.sharding import PartitionSpec as P

epsilon = 1e-06
MESH = pl.DeviceIdType.MESH
LANES = 128
f32, bf16 = jnp.float32, jnp.bfloat16


def silu_norm(values, gain):
    inverse = lax.rsqrt(jnp.mean(values * values, axis=-1, keepdims=True) + epsilon)
    return jax.nn.silu(values * inverse * gain)


def kernel(sizes, *refs):
    placed, out, scratch = refs[:8], refs[8], refs[9:]
    n_t, n_z, n_w = sizes
    cnt_ref, feat_hbm, g1_hbm, w1_hbm, b1_hbm, g2_hbm, w2_hbm, b2_hbm = placed
    (feat, g1, b1, g2, b2, wl1, wc1, ws1, wl2, wc2, ws2, lsem, lo1, hc1, hs1, lo2, hc2, hs2, acc,
     clo, chc, chs, cnt_own, cnt_in, carry, carry_col,
     raw_in, rows1, col_out1, col_in1, tail1, tailc1, tail_in1, tailc_in1, tailhc_in,
     rows2, col_out2, col_in2, tail2, tailc2, taile2, tail_in2, tailc_in2, taile_in2,
     nsend, nrecv, fsend, frecv, up, over, over_up) = scratch
    F, R, X, C = feat.shape
    H = F // 2
    S = F * X
    T = 2 * X
    me_t, me_z, me_w = lax.axis_index("tchunk"), lax.axis_index("ha"), lax.axis_index("wa")
    left_core = me_w == 0
    has = (me_z > 0, me_z < n_z - 1)
    frame_of = [(g % 2) * H + g // 2 for g in range(F)]

    def load(i, src, dst):
        return pltpu.make_async_copy(src, dst, lsem.at[i])

    def weight_loads(i, w, wl, wc, ws):
        low, high = pl.ds(0, LANES), pl.ds(LANES, C - LANES)
        top, bottom = pl.ds(0, C - LANES), pl.ds(C - LANES, C - LANES)
        return [
            load(i, w.at[:, :, :, low], wl),
            load(i + 1, w.at[0, :, 1, high], wc.at[0, :, top]),
            load(i + 2, w.at[1, :, 1, high], wc.at[0, :, bottom]),
            load(i + 3, w.at[2, :, 1, high], wc.at[1, :, top]),
            load(i + 4, w.at[:, :, 0, high], ws.at[:, :, top]),
            load(i + 5, w.at[:, :, 2, high], ws.at[:, :, bottom]),
        ]

    load_feat = load(0, feat_hbm, feat)
    load_g1 = load(1, g1_hbm, g1)
    load_rest = [load(2, b1_hbm, b1), load(3, g2_hbm, g2), load(4, b2_hbm, b2)]
    load_w1 = weight_loads(5, w1_hbm, wl1, wc1, ws1)
    load_w2 = weight_loads(11, w2_hbm, wl2, wc2, ws2)
    load_feat.start()
    load_g1.start()

    def device(k, dz, flip):
        return {
            "tchunk": k,
            "ha": lax.rem(me_z + dz + n_z, n_z),
            "wa": 1 - me_w if flip else me_w,
        }

    barrier = pltpu.get_barrier_semaphore()

    def greet(k, dz, flip):
        pl.semaphore_signal(barrier, inc=1, device_id=device(k, dz, flip), device_id_type=MESH)

    greet(me_t, 0, True)

    @pl.when(has[1])
    def _():
        greet(me_t, 1, False)
        greet(me_t, 1, True)

    for k in range(1, n_t):
        @pl.when(me_t < k)
        def _(k=k):
            greet(k, 0, False)

    expected = 1 + 2 * has[0].astype(jnp.int32) + me_t

    def tell(sem, k, dz, flip):
        pl.semaphore_signal(sem, inc=1, device_id=device(k, dz, flip), device_id_type=MESH)

    def tell_lower(sems):
        for k in range(1, n_t):
            @pl.when(me_t == k)
            def _(k=k):
                for lower in range(k):
                    tell(sems.at[k], lower, 0, False)

    for c in load_w1 + load_rest + load_w2:
        c.start()

    def remote(src, dst, ssem, rsem, to):
        return pltpu.make_async_remote_copy(src, dst, ssem, rsem, device_id=to, device_id_type=MESH)

    def row_copy(side, way=1):
        src = feat_hbm.at[:, pl.ds((R - 2) * side, 2)]
        return remote(src, raw_in.at[1 - side], nsend.at[side], nrecv.at[side], device(me_t, way * (2 * side - 1), False))

    def corner_copy(side, way=1):
        src = col_out1.at[pl.ds((R - 2) * side, 2)]
        dst = col_in1.at[pl.ds(0 if side else R + 2, 2)]
        i = 2 + side
        return remote(src, dst, nsend.at[i], nrecv.at[i], device(me_t, way * (2 * side - 1), True))

    def col_copy(first):
        src, dst, i = (col_out1, col_in1.at[pl.ds(2, R)], 4) if first else (col_out2, col_in2, 5)
        return remote(src, dst, nsend.at[i], nrecv.at[i], device(me_t, 0, True))

    def far(k, slot, i, way=1):
        src, dst, dz, flip = (
            (tail1, tail_in1.at[slot, pl.ds(0, R)], 0, False),
            (tailc1, tailc_in1.at[slot], 0, True),
            (tail1.at[pl.ds(0, 2)], tail_in1.at[slot, pl.ds(R + 2, 2)], -1, False),
            (tailc1, tailhc_in.at[slot, 1], -1, True),
            (tail1.at[pl.ds(R - 2, 2)], tail_in1.at[slot, pl.ds(R, 2)], 1, False),
            (tailc1, tailhc_in.at[slot, 0], 1, True),
            (tail2.at[pl.ds(0, R - 2)], tail_in2.at[slot, pl.ds(0, R - 2)], 0, False),
            (tailc2, tailc_in2.at[slot], 0, True),
            (cnt_own, cnt_in.at[slot], 0, False),
            (tail2.at[pl.ds(R - 2, 4)], tail_in2.at[slot, pl.ds(R - 2, 4)], 0, False),
            (taile2, taile_in2.at[slot], 0, True),
        )[i]
        return remote(src, dst, fsend.at[k, i], frecv.at[slot, i], device(k, way * dz, flip))

    def later(act):
        for k in range(1, n_t):
            @pl.when(me_t < k)
            def _(k=k):
                act(k)

    def aside(act, side):
        @pl.when(has[side])
        def _():
            for i in (2, 3) if side == 0 else (4, 5):
                act(i)

    for side in range(2):
        @pl.when(jnp.logical_not(has[side]))
        def _(side=side):
            raw_in[side] = jnp.zeros((F, 2, X, C), bf16)
            col_in1[pl.ds(side * (R + 2), 2)] = jnp.zeros((2, F, C), bf16)
            for k in range(n_t - 1):
                tail_in1[k, pl.ds(R + 2 * side, 2)] = jnp.zeros((2, T, C), bf16)
                tailhc_in[k, side] = jnp.zeros((2, R, C), bf16)
    for wc in (wc1, wc2):
        wc[1, :, C - LANES :] = jnp.zeros((3, C - LANES, C), bf16)

    count = cnt_ref[0]
    cnt_own[...] = jnp.full(cnt_own.shape, count.astype(f32), f32)
    group = lax.broadcasted_iota(jnp.int32, (F, X, C), 0)
    live = lax.rem(group, 2) * H + group // 2 < count

    def edge(v, at=0):
        return jnp.where(left_core, v[:, at + X - 1, :], v[:, at, :])

    def tail_of(v):
        got = []
        for f in range(2):
            t = jnp.zeros((X, C), f32)
            for g in range(F):
                t = jnp.where(count - 2 + f == frame_of[g], v[g], t)
            got.append(t)
        return jnp.concatenate(got, axis=0).astype(bf16)

    def slot_of(h):
        return h - 2 if 2 <= h < R else R - 2 + h if h < 2 else h

    def put_tail_cols(tails, dst):
        v = tails[...].astype(f32)
        more = dst.shape[1] - v.shape[0]
        for f in range(2):
            c = edge(v, f * X)
            if more:
                c = jnp.concatenate([c, jnp.zeros((more, C), f32)], axis=0)
            dst[f] = c.astype(bf16)

    def tiles(b):
        zero = jnp.zeros((X, C), f32)
        front = jnp.concatenate([zero, b[2 * (H - 2)], zero, b[2 * (H - 1)]], axis=0)
        return jnp.concatenate([front, b.reshape(S, C)], axis=0).astype(bf16)

    tiles1, tiles2 = (lo1, hc1, hs1), (lo2, hc2, hs2)

    def center(into, yy, v):
        lo, hc, _ = into
        t = tiles(v)
        lo[1, yy] = t[:, :LANES]
        high = t[:, LANES:]
        after = jnp.concatenate([high[T:], jnp.zeros((T, C - LANES), bf16)], axis=0)
        hc[yy] = jnp.concatenate([high, after], axis=1)

    def beside(v, col):
        index = lax.broadcasted_iota(jnp.int32, v.shape, 1)
        none = jnp.zeros(col.shape, f32)
        lcol = jnp.where(left_core, none, col)
        rcol = jnp.where(left_core, col, none)
        left = jnp.where(index == 0, jnp.broadcast_to(lcol[:, None, :], v.shape), pltpu.roll(v, 1, 1))
        right = jnp.where(index == X - 1, jnp.broadcast_to(rcol[:, None, :], v.shape), pltpu.roll(v, X - 1, 1))
        return left, right

    def sides(into, yy, v, col):
        lo, _, hs = into
        left, right = beside(v, col)
        tl, tr = tiles(left), tiles(right)
        lo[0, yy] = tl[:, :LANES]
        lo[2, yy] = tr[:, :LANES]
        hs[yy] = jnp.concatenate([tl[:, LANES:], tr[:, LANES:]], axis=1)

    def grouped(ref, index):
        return jnp.concatenate([ref[(t,) + index].astype(f32)[None] for t in frame_of], axis=0)

    def as_groups(ref, y):
        return ref[y].astype(f32).reshape(F, X, C)

    def conv(of, y0, n, wl, wc, ws, part=None, taps=(0, 1, 2), add=False):
        lo, hc, hs = of

        def take(ref, i, a):
            return ref[pl.ds(y0 + i, n), pl.ds(a * T, S)].reshape(n * S, LANES)

        lhs, rhs = [], []
        for i in taps:
            if part != "sides":
                lhs += [take(lo.at[1], i, a) for a in range(3)] + [take(hc, i, 0), take(hc, i, 2)]
                rhs += [wl[a, i, 1] for a in range(3)] + [wc[0, i], wc[1, i]]
            if part != "center":
                lhs += [take(lo.at[j], i, a) for a in range(3) for j in (0, 2)] + [take(hs, i, a) for a in range(3)]
                rhs += [wl[a, i, j] for a in range(3) for j in (0, 2)] + [ws[a, i] for a in range(3)]
        got = jnp.dot(jnp.concatenate(lhs, axis=1), jnp.concatenate(rhs, axis=0), preferred_element_type=f32)
        if part == "sides" or add:
            acc[pl.ds(y0 * S, n * S)] += got
        else:
            acc[pl.ds(y0 * S, n * S)] = got

    def before(first, n, wl, wc, ws):
        tail_in = tail_in1 if first else tail_in2
        col_refs = (tailc_in1, tailhc_in.at[:, 0], tailhc_in.at[:, 1]) if first else (tailc_in2, taile_in2)

        def arrive(k):
            for i in (8, 0, 1) if first else (6, 7, 9, 10):
                far(k, k, i).wait_recv()
            if first:
                @pl.when(has[0])
                def _():
                    for i in (4, 5):
                        far(k, k, i, -1).wait_recv()

                @pl.when(has[1])
                def _():
                    for i in (2, 3):
                        far(k, k, i, -1).wait_recv()

        arrive(0)
        if n_t > 2:
            for at in range(n + 2):
                carry[at] = tail_in[0, at].astype(f32)
            for d, ref in enumerate(col_refs):
                late = ref[0].astype(f32)
                carry_col[d, :, : late.shape[1]] = late
        for k in range(1, n_t - 1):
            @pl.when(me_t > k)
            def _(k=k):
                arrive(k)
                total = cnt_in[k]

                def merge(total, early0, early1, late0, late1):
                    both, some = total > 1.5, total > 0.5
                    return (
                        jnp.where(both, late0, jnp.where(some, early1, early0)),
                        jnp.where(some, late1, early1),
                    )

                for at in range(n + 2):
                    late = tail_in[k, at].astype(f32)
                    got = merge(total, carry[at, :X], carry[at, X:], late[:X], late[X:])
                    carry[at] = jnp.concatenate(got, axis=0)
                for d, ref in enumerate(col_refs):
                    late = ref[k].astype(f32)
                    there = pl.ds(0, late.shape[1])
                    got = merge(total[:1], carry_col[d, 0, there], carry_col[d, 1, there], late[0], late[1])
                    carry_col[d, 0, there] = got[0]
                    carry_col[d, 1, there] = got[1]

        if n_t > 2:
            cols = [carry_col[d] for d in range(len(col_refs))]
        else:
            cols = [ref[0].astype(f32) for ref in col_refs]
        zero = jnp.zeros((X, C), f32)
        for yy in range(n + 2):
            at = slot_of(yy)
            d, y = (0, at) if at < R - 2 else (1, at - R + 2)
            if first:
                if yy < 2:
                    at, d, y = R + yy, 1, R - 2 + yy
                elif yy < R + 2:
                    at, d, y = yy - 2, 0, yy - 2
                else:
                    d, y = 2, yy - R - 2
            col = jnp.concatenate([cols[d][f, y : y + 1] for f in range(2)], axis=0)
            v = (carry[at] if n_t > 2 else tail_in[0, at].astype(f32)).reshape(2, X, C)
            left, right = beside(v, col)
            made = []
            for j, b in enumerate((left, v, right)):
                t = jnp.concatenate([b[0], b[1], b[1], zero], axis=0).astype(bf16)
                clo[j, yy] = t[:, :LANES]
                made.append(t[:, LANES:])
            chs[yy] = jnp.concatenate([made[0], made[2]], axis=1)
            chc[yy] = jnp.concatenate([made[1][:T], made[1][T:]], axis=1)
        lhs, rhs = [], []
        for i in range(3):
            for a in range(2):
                for j in range(3):
                    lhs.append(clo[j, pl.ds(i, n), pl.ds(a * T, T)].reshape(n * T, LANES))
                lhs.append(chs[pl.ds(i, n), pl.ds(a * T, T)].reshape(n * T, LANES))
                rhs += [wl[a, i].reshape(3 * LANES, C), ws[a, i]]
            lhs.append(chc[pl.ds(i, n)].reshape(n * T, LANES))
            rhs.append(wc[0, i])
        part = jnp.dot(jnp.concatenate(lhs, axis=1), jnp.concatenate(rhs, axis=0), preferred_element_type=f32)
        for y in range(n):
            for f in range(2):
                acc[pl.ds(y * S + f * T, X)] += part[y * T + f * X : y * T + (f + 1) * X]

    pl.semaphore_wait(barrier, expected)
    tell_lower(over)

    @pl.when(has[0])
    def _():
        tell(up.at[0], me_t, -1, False)
        tell(up.at[1], me_t, -1, True)
        row_copy(0).start()

    load_feat.wait()
    load_g1.wait()

    def keep_first(y):
        v = silu_norm(grouped(feat, (y,)), g1[...].reshape(1, 1, C))
        v = jnp.where(live, v, 0.0)
        rows1[y] = v.reshape(S, C).astype(bf16)
        col_out1[y] = edge(v).astype(bf16)
        center(tiles1, y + 2, v)

    ends = sorted({0, 1, R - 2, R - 1})
    for y in ends:
        keep_first(y)

    @pl.when(has[0])
    def _():
        corner_copy(0).start()

    for y in range(R):
        if y not in ends:
            keep_first(y)
    col_copy(True).start()

    @pl.when(has[1])
    def _():
        pl.semaphore_wait(up.at[0], 1)
        row_copy(1).start()
        pl.semaphore_wait(up.at[1], 1)
        corner_copy(1).start()
        tell_lower(over_up)

    if n_t > 1:
        @pl.when(me_t < n_t - 1)
        def _():
            for y in range(R):
                tail1[y] = tail_of(as_groups(rows1, y))
            put_tail_cols(tail1, tailc1)

        def tails_first(k):
            pl.semaphore_wait(over.at[k], 1)
            for i in (8, 0, 1):
                far(k, me_t, i).start()
            aside(lambda i: far(k, me_t, i).start(), 0)

        def tails_up(k):
            @pl.when(has[1])
            def _():
                pl.semaphore_wait(over_up.at[k], 1)
                for i in (4, 5):
                    far(k, me_t, i).start()

        later(tails_first)
    col_copy(True).wait_recv()
    for y in range(R):
        sides(tiles1, y + 2, as_groups(rows1, y), col_in1[y + 2].astype(f32))
    if n_t > 1:
        @pl.when(me_z > 0)
        def _():
            later(tails_up)

    for c in load_w1:
        c.wait()
    half = (R - 2) // 2
    conv(tiles1, 2, half, wl1, wc1, ws1)
    conv(tiles1, 2 + half, R - 2 - half, wl1, wc1, ws1)
    conv(tiles1, 0, 2, wl1, wc1, ws1, taps=(2,))
    conv(tiles1, R, 2, wl1, wc1, ws1, taps=(0,))
    if n_t > 1:
        @pl.when(me_z == 0)
        def _():
            later(tails_up)

    for c in load_rest:
        c.wait()

    def second(h, groups):
        v = silu_norm(acc[pl.ds(h * S, groups * X)] + b1[...], g2[...]).reshape(groups, X, C)
        v = jnp.where(live[:groups], v, 0.0)
        if h in (0, R + 1):
            v = jnp.where(has[min(h, 1)], v, 0.0)
        rows2[h, : groups * X] = v.reshape(groups * X, C).astype(bf16)
        return v

    def keep_second(h, v):
        col_out2[h] = edge(v).astype(bf16)
        center(tiles2, h, v)

    def put_tails(rows, at, n, dst):
        for h in rows:
            tail2[slot_of(h)] = tail_of(as_groups(rows2, h))
        put_tail_cols(tail2.at[pl.ds(at, n)], dst)

    def tails_second(which):
        def act(k):
            for i in which:
                far(k, me_t, i).start()

        return act

    for h in range(2, R):
        keep_second(h, second(h, F))
    if n_t > 1:
        @pl.when(me_t == 0)
        def _():
            put_tails(range(2, R), 0, R - 2, tailc2)
            later(tails_second((6, 7)))

    for side in range(2):
        @pl.when(has[side])
        def _(side=side):
            row_copy(1 - side, -1).wait_recv()
            corner_copy(1 - side, -1).wait_recv()
    for side in range(2):
        for r in range(2):
            v = silu_norm(grouped(raw_in.at[side], (r,)), g1[...].reshape(1, 1, C))
            v = jnp.where(live, v, 0.0)
            yy = side * (R + 2) + r
            v = v.astype(bf16).astype(f32)
            center(tiles1, yy, v)
            sides(tiles1, yy, v, col_in1[yy].astype(f32))
    conv(tiles1, 0, 2, wl1, wc1, ws1, taps=(0, 1), add=True)
    conv(tiles1, R, 2, wl1, wc1, ws1, taps=(1, 2), add=True)
    ends = (0, 1, R, R + 1)

    @pl.when(me_t == 0)
    def _():
        for h in ends:
            keep_second(h, second(h, F))
        if n_t > 1:
            put_tails(ends, R - 2, 4, taile2)
            later(tails_second((9, 10)))

    if n_t > 1:
        @pl.when(me_t > 0)
        def _():
            before(True, R + 2, wl1, wc1, ws1)
            for h in ends:
                keep_second(h, second(h, F))
            for h in range(2, R):
                v = second(h, 4)
                rest = rows2[h, 4 * X :].astype(f32).reshape(F - 4, X, C)
                v = jnp.concatenate([v, rest], axis=0)
                col_out2[h] = edge(v).astype(bf16)
                t = jnp.concatenate([jnp.zeros((X, C), f32), v[2 * (H - 1)], v[:6].reshape(6 * X, C)], axis=0)
                t = t.astype(bf16)
                high = t[:, LANES:]
                lo2[1, h, 2 * T : 4 * T] = t[T : 3 * T, :LANES]
                hc2[h, T : 4 * T] = jnp.concatenate([high[: 3 * T], high[T:]], axis=1)
            if n_t > 2:
                @pl.when(me_t < n_t - 1)
                def _():
                    put_tails(range(2, R), 0, R - 2, tailc2)
                    put_tails(ends, R - 2, 4, taile2)
                    later(tails_second((6, 7, 9, 10)))

    col_copy(False).start()

    for c in load_w2:
        c.wait()
    for y in (0, R // 2):
        conv(tiles2, y, R // 2 if y == 0 else R - R // 2, wl2, wc2, ws2, "center")
    col_copy(False).wait_recv()
    for h in range(R + 2):
        sides(tiles2, h, as_groups(rows2, h), col_in2[h].astype(f32))
    for y in (0, R // 2):
        conv(tiles2, y, R // 2 if y == 0 else R - R // 2, wl2, wc2, ws2, "sides")
    if n_t > 1:
        @pl.when(me_t > 0)
        def _():
            before(False, R, wl2, wc2, ws2)

    for y in range(R):
        result = acc[pl.ds(y * S, S)] + b2[...]
        for g in range(F):
            t = frame_of[g]
            value = feat[t, y].astype(f32) + result[g * X : (g + 1) * X]
            out[t, y] = jnp.where(live[g], value, 0.0).astype(bf16)

    col_copy(True).wait_send()
    col_copy(False).wait_send()
    for side in range(2):
        @pl.when(has[side])
        def _(side=side):
            row_copy(side).wait_send()
            corner_copy(side).wait_send()

    def sent(k):
        for i in (8, 0, 1, 6, 7, 9, 10):
            far(k, me_t, i).wait_send()
        for side in range(2):
            aside(lambda i: far(k, me_t, i).wait_send(), side)

    later(sent)


def shards(sizes, features, frame_counts, gain_first, conv_first, bias_first, gain_second, conv_second, bias_second):
    F, R, X, C = features.shape
    n_t, n_z, n_w = sizes
    assert n_w == 2 and F % 2 == 0 and F >= 6 and X == 8 and 2 * (C - LANES) == LANES and R >= 4
    H = F // 2
    S, T = F * X, 2 * X
    inner = -(-(R - 2) // 8) * 8
    dma = pltpu.SemaphoreType.DMA
    V = pltpu.VMEM
    weights = [V((3, 3, 3, LANES, C), bf16), V((2, 3, LANES, C), bf16), V((3, 3, LANES, C), bf16)]
    scratch = [
        V(features.shape, bf16),
        V((1, C), f32),
        V((1, C), f32),
        V((1, C), f32),
        V((1, C), f32),
        *weights,
        *weights,
        dma((17,)),
        V((3, R + 4, (H + 2) * T, LANES), bf16),
        V((R + 4, (H + 2) * T, LANES), bf16),
        V((R + 4, (H + 2) * T, LANES), bf16),
        V((3, R + 2, (H + 2) * T, LANES), bf16),
        V((R + 2, (H + 2) * T, LANES), bf16),
        V((R + 2, (H + 2) * T, LANES), bf16),
        V(((R + 2) * S, C), f32),
        V((3, R + 4, 2 * T, LANES), bf16),
        V((R + 4, T, LANES), bf16),
        V((R + 4, 2 * T, LANES), bf16),
        V((X, C), f32),
        V((n_t, X, C), f32),
        V((R + 4, T, C), f32),
        V((3, 2, max(R, inner, 8), C), f32),
        V((2, F, 2, X, C), bf16),
        V((R, S, C), bf16),
        V((R, F, C), bf16),
        V((R + 4, F, C), bf16),
        V((R, T, C), bf16),
        V((2, R, C), bf16),
        V((n_t, R + 4, T, C), bf16),
        V((n_t, 2, R, C), bf16),
        V((n_t, 2, 2, R, C), bf16),
        V((R + 2, S, C), bf16),
        V((R + 2, F, C), bf16),
        V((R + 2, F, C), bf16),
        V((R + 2, T, C), bf16),
        V((2, inner, C), bf16),
        V((2, 8, C), bf16),
        V((n_t, R + 2, T, C), bf16),
        V((n_t, 2, inner, C), bf16),
        V((n_t, 2, 8, C), bf16),
        dma((6,)),
        dma((6,)),
        dma((n_t, 11)),
        dma((n_t, 11)),
        pltpu.SemaphoreType.REGULAR((2,)),
        pltpu.SemaphoreType.REGULAR((n_t,)),
        pltpu.SemaphoreType.REGULAR((n_t,)),
    ]
    return pl.pallas_call(
        functools.partial(kernel, sizes),
        out_shape=pltpu.VMEM(features.shape, features.dtype),
        in_specs=[pl.BlockSpec(memory_space=pltpu.SMEM)] + [pl.BlockSpec(memory_space=pltpu.HBM)] * 7,
        out_specs=pl.BlockSpec(memory_space=pltpu.VMEM),
        scratch_shapes=scratch,
        compiler_params=pltpu.CompilerParams(
            collective_id=0, has_side_effects=True, vmem_limit_bytes=58 << 20
        ),
    )(
        frame_counts,
        features,
        gain_first.reshape(1, C),
        conv_first,
        bias_first.reshape(1, C),
        gain_second.reshape(1, C),
        conv_second,
        bias_second.reshape(1, C),
    )


def solution(mesh):
    sizes = (mesh.shape["tchunk"], mesh.shape["ha"], mesh.shape["wa"])
    spec = P(("grp", "tchunk"), "ha", "wa", None)
    return jax.shard_map(
        functools.partial(shards, sizes),
        mesh=mesh,
        in_specs=(spec, P(("grp", "tchunk")), P(), P(), P(), P(), P(), P()),
        out_specs=spec,
        check_vma=False,
    )
```
